32 devices in a mesh: layer: 4 (over x, core), row: 4 (over z), col: 2 (over y).
Axes of the slice: x: 2, y: 2, z: 4, core: 2. Of those that a mesh axis runs over, the one named last changes fastest.
Arguments:
- sources: bfloat16 [4, 96, 12288], P('layer', 'col', 'row'), may hold values from -6 to 6
- transmission: bfloat16 [4, 12288, 12288], P('layer', 'row', 'col'), may hold values from -0.0546875 to 0.0546875
- reflection: bfloat16 [4, 12288, 12288], P('layer', 'row', 'col'), may hold values from -0.02734375 to 0.02734375
Outputs:
- upgoing: bfloat16 [4, 96, 12288], P('layer', 'col', 'row')
The draws below stay inside these ranges and needn't reach their ends.
All inputs are finite; a program needn't handle non-finite values.
Results may differ from the reference program's by a relative error of at most 0.012.
Values may be sent and summed in bfloat16 or wider, within the bound.
A program may use at most 128 MiB of HBM per device.

```python
import jax
import jax.numpy as jnp
from jax import lax

M = 12288
TRACES = 96
LAYERS = 4


def block_levels(own_key, dims, shards, smallest, high):
    gain, own = 1.0, jax.random.fold_in(own_key, 6)
    for position, shards_of in shards:
        steps = jnp.exp(jax.random.uniform(jax.random.fold_in(own, position), (shards_of,), jnp.float32, smallest / len(shards), high / len(shards)))
        gain = gain * jnp.repeat(steps, dims[position] // shards_of).reshape([-1 if axis == position else 1 for axis in range(len(dims))])
    return gain


def normal_values(rng, dims, spread, limit, shards=(), dtype=jnp.bfloat16):
    gain = block_levels(rng, dims, shards, -0.22, 0.18) if shards else 1.0
    entries = jax.random.normal(rng, dims, jnp.float32) * spread * gain
    return jnp.minimum(jnp.maximum(entries, -limit), limit).astype(dtype)


def setup_inputs(seed: int = 0) -> dict:
    key_of = jax.random.split(jax.random.key(seed), 4)
    sources = normal_values(key_of[0], (LAYERS, TRACES, M), 1.0, 6.0, ((0, 4), (1, 2), (2, 4)))
    transmission = normal_values(key_of[1], (LAYERS, M, M), M ** -0.5, 0.0546875, ((0, 4), (1, 4), (2, 2)))
    reflection = normal_values(key_of[2], (LAYERS, M, M), (4 * M) ** -0.5, 0.02734375, ((0, 4), (1, 4), (2, 2)))
    return {"sources": sources, "transmission": transmission, "reflection": reflection}


def reference(sources, transmission, reflection):
    down = jnp.zeros((TRACES, M), jnp.bfloat16)
    incidents = []
    for level in range(LAYERS):
        incident = (down.astype(jnp.float32) + sources[level].astype(jnp.float32)).astype(jnp.bfloat16)
        incidents.append(incident)
        down = jnp.dot(incident, transmission[level], preferred_element_type=jnp.float32).astype(jnp.bfloat16)
    upward = down
    results = [None] * LAYERS
    for level in reversed(range(LAYERS)):
        passed = lax.dot_general(upward, transmission[level], (((1,), (1,)), ((), ())), preferred_element_type=jnp.float32)
        bounced = lax.dot_general(incidents[level], reflection[level], (((1,), (1,)), ((), ())), preferred_element_type=jnp.float32)
        upward = (passed + bounced).astype(jnp.bfloat16)
        results[level] = upward
    return jnp.stack(results)
```

```python
import functools

import jax
import jax.numpy as jnp
from jax import lax
from jax.experimental import pallas as pl
from jax.experimental.pallas import tpu as pltpu
from jax.sharding import PartitionSpec as P

MESH = pl.DeviceIdType.MESH
BF16 = jnp.bfloat16
F32 = jnp.float32


def kernel(
    layers, rows, cols, r_tile,
    src_ref, trans_ref, refl_ref, out_ref,
    tv, rbuf, ssend, sp, incn, pbuf, rel, zbuf, incp, ginc, gup, acc, ubuf, urec, natu, obuf,
    t_sem, r_sem, s_send, s_recv, i_send, i_recv, d_send, rel_recv, f_send, z_recv,
    n_send, n_recv, g_send, g_recv, u_send, u_recv, o_send, o_recv,
):
    ratio = rows // cols
    half = layers // 2
    pieces = 2 * cols
    chunks = ratio * pieces
    lay, row, col = (lax.axis_index(name) for name in ("layer", "row", "col"))
    part, cw = pbuf.shape[2], pbuf.shape[3]
    traces = cols * part
    per = cw // r_tile
    last = layers - 1
    home_col, home_b = lax.div(row, ratio), lax.rem(row, ratio)

    def other(index, by, size):
        return lax.rem(index + by, size)

    def peer(layer):
        return lax.rem(layer + half, layers)

    def holder(layer, k):
        return lax.rem(layer + k * half, layers)

    def plane(layer):
        return lax.div(layer, half)

    def remote(src, dst, send, recv, target):
        return pltpu.make_async_remote_copy(
            src_ref=src, dst_ref=dst, send_sem=send, recv_sem=recv,
            device_id=target, device_id_type=MESH,
        )

    me = (lay, row, col)
    up_peer = lax.rem(lay + 1, layers)

    def arrival(dst, recv):
        return remote(dst, dst, recv, recv, (up_peer, row, col))

    base = jnp.where(lay < last, lay + 1, last - 1)
    near_k = jnp.where(plane(base) == plane(lay), 0, 1)

    def order(step):
        o, b = lax.div(step, ratio), lax.rem(step, ratio)
        near = lax.div(o, cols)
        d = cols - 1 - lax.rem(o, cols)
        k = jnp.where(near == 1, near_k, 1 - near_k)
        y = other(col, d, cols)
        return near, d, k, y, b, k * cols + y

    def t_copy(j):
        start = pl.multiple_of(j * cw, 128)
        return pltpu.make_async_copy(trans_ref.at[:, pl.ds(start, cw)], tv.at[j], t_sem.at[j])

    def r_index(step):
        p, b = lax.div(step, ratio), lax.rem(step, ratio)
        return b, p

    def r_copy(step):
        b, p = r_index(step)
        start = pl.multiple_of((b * pieces + p) * cw, 128)
        slot = lax.rem(step, 2)
        return pltpu.make_async_copy(
            refl_ref.at[:, pl.ds(start, cw)], rbuf.at[slot], r_sem.at[slot]
        )

    for step in range(chunks):
        b, p = order(step)[-2:]
        t_copy(b * pieces + p).start()

    barrier = pltpu.get_barrier_semaphore()
    for dl in range(layers):
        for dr in range(rows):
            for dc in range(cols):
                if dl or dr or dc:
                    pl.semaphore_signal(
                        barrier, inc=1, device_id_type=MESH,
                        device_id=(other(lay, dl, layers), other(row, dr, rows), other(col, dc, cols)),
                    )
    pl.semaphore_wait(barrier, layers * rows * cols - 1)

    for k in range(2):
        for y in range(cols):
            p = k * cols + y
            ssend[p] = src_ref[:, p * cw:(p + 1) * cw]

    def first_copy(c, p):
        return remote(ssend.at[p], incn.at[p, col], i_send.at[c, p], i_recv.at[col, p], (lay, row, c))

    @pl.when(lay == 0)
    def _():
        for p in range(pieces):
            for d in range(1, cols):
                first_copy(other(col, d, cols), p).start()
            incn[p, col] = ssend[p]

    def s_copy(k, y):
        return remote(ssend.at[k * cols + y], sp.at[k, col], s_send.at[k, y], s_recv.at[k, col],
                      (holder(lay, k), row, y))

    for k in (1, 0):
        for d in range(cols):
            if k or d:
                s_copy(k, other(col, d, cols)).start()
    sp[0, col] = ssend[col]
    acc[...] = jnp.zeros_like(acc)

    def got_s(k):
        for d in range(cols):
            if k or d:
                c = other(col, d, cols)
                arrival(sp.at[k, c], s_recv.at[k, c]).wait_recv()

    def g_copy(slot, block, buf, which, k, layer, r):
        return remote(block, buf.at[home_b, k * cols + col], g_send.at[slot, r],
                      g_recv.at[which, home_b, k * cols + col], (layer, r, home_col))

    def spread(slot, block, buf, which, k, layer):
        for d in range(1, rows):
            g_copy(slot, block, buf, which, k, layer, other(row, d, rows)).start()
        mine = (layer == lay) & (home_col == col)

        @pl.when(mine)
        def _():
            buf[home_b, k * cols + col] = block[...]

        @pl.when(jnp.logical_not(mine))
        def _():
            g_copy(slot, block, buf, which, k, layer, row).start()

    def spread_sent(slot, block, buf, which, k, layer):
        for d in range(1, rows):
            g_copy(slot, block, buf, which, k, layer, other(row, d, rows)).wait_send()

        @pl.when(jnp.logical_not((layer == lay) & (home_col == col)))
        def _():
            g_copy(slot, block, buf, which, k, layer, row).wait_send()

    def arrived_g(which, b, p):
        buf = gup if which else ginc
        if which:
            arrival(buf.at[b, p], g_recv.at[which, b, p]).wait_recv()
            return
        mine = (ratio * col + b == row) & (p == col)

        @pl.when(jnp.logical_not(mine))
        def _():
            arrival(buf.at[b, p], g_recv.at[which, b, p]).wait_recv()

    for k in range(2):
        @pl.when(lay == k * half)
        def _():
            got_s(k)
            incp[k] = sp[k]
            spread(k, incp.at[k], ginc, 0, k, 0)

    def d_copy(step):
        near, d, k, y, b, p = order(step)
        j = b * pieces + p
        q = jnp.where(lay == last, 2, k)
        target = holder(base, k)
        direct = (near == 1) & (d == 0)
        return direct, remote(
            pbuf.at[j], zbuf.at[q, row], d_send.at[j], z_recv.at[q, row],
            (target, ratio * col + b, col),
        ), remote(
            pbuf.at[j], rel.at[q, col, b], d_send.at[j], rel_recv.at[q, col, b], (target, row, y),
        )

    def down_compute():
        @pl.when(lay == 0)
        def _():
            for p in range(pieces):
                for d in range(1, cols):
                    c = other(col, d, cols)
                    arrival(incn.at[p, c], i_recv.at[c, p]).wait_recv()

        @pl.when(lay > 0)
        def _():
            for k in range(2):
                for d in range(cols):
                    if k or d:
                        p = k * cols + other(col, d, cols)
                        arrival(incn.at[p], n_recv.at[p]).wait_recv()

        def down_step(step, carry):
            b, p = order(step)[-2:]
            j = b * pieces + p
            t_copy(j).wait()
            total = jnp.zeros((traces, cw), F32)
            for i in range(pieces):
                total += jnp.dot(
                    incn[i].reshape(traces, cw), tv[j, pl.ds(i * cw, cw), :],
                    preferred_element_type=F32,
                )
            pbuf[j] = total.astype(BF16).reshape(cols, part, cw)
            direct, straight, relayed = d_copy(step)

            @pl.when(direct)
            def _():
                straight.start()

            @pl.when(jnp.logical_not(direct))
            def _():
                relayed.start()

            return carry

        lax.fori_loop(0, chunks, down_step, 0)
        for step in range(2):
            r_copy(step).start()

    def f_copy(q, c, b):
        goal = ratio * c + b
        return goal, remote(rel.at[q, c, b], zbuf.at[q, row], f_send.at[q, c, b], z_recv.at[q, row],
                            (lay, goal, col))

    def n_copy(k, layer, c):
        p = k * cols + col
        return remote(incp.at[k], incn.at[p], n_send.at[k, c], n_recv.at[p], (layer, row, c))

    def forward(q, c):
        for b in range(ratio):
            arrival(rel.at[q, c, b], rel_recv.at[q, c, b]).wait_recv()
            goal, copy = f_copy(q, c, b)

            @pl.when(goal == row)
            def _():
                zbuf[q, row] = rel[q, c, b]

            @pl.when(goal != row)
            def _():
                copy.start()

    def down_sum(l, m, k):
        q = jnp.where(l == last, 2, k)
        same = plane(l) == plane(lay)
        for d in range(1, cols):
            forward(q, other(col, d, cols))

        @pl.when(jnp.logical_not(same))
        def _():
            forward(q, col)

        for d in range(rows):
            r = other(row, d, rows)
            if d:
                arrival(zbuf.at[q, r], z_recv.at[q, r]).wait_recv()
            else:
                @pl.when(same & (home_col == col))
                def _():
                    arrival(zbuf.at[q, r], z_recv.at[q, r]).wait_recv()

        @pl.when(l < last)
        def _():
            for c in range(cols):
                down = jnp.sum(zbuf[q, :, c].astype(F32), axis=0).astype(BF16)
                incp[k, c] = (down.astype(F32) + sp[k, c].astype(F32)).astype(BF16)
            for c in range(cols):
                mine = (k == 0) & (col == c)

                @pl.when(mine)
                def _():
                    incn[k * cols + col] = incp[k]

                @pl.when(jnp.logical_not(mine))
                def _():
                    n_copy(k, m, c).start()

            spread(k, incp.at[k], ginc, 0, k, m)

        @pl.when(l == last)
        def _():
            for c in range(cols):
                incp[2, c] = jnp.sum(zbuf[2, :, c].astype(F32), axis=0).astype(BF16)
            spread(2, incp.at[2], gup, 1, k, last)

    contract = (((1,), (1,)), ((), ()))

    def times(lhs, rhs):
        return lax.dot_general(lhs, rhs, contract, preferred_element_type=F32)

    def reflect():
        def reflect_step(step, carry):
            b, p = r_index(step)
            arrived_g(0, b, p)
            r_copy(step).wait()
            lhs = ginc[b, p].reshape(traces, cw)
            slot = lax.rem(step, 2)
            for i in range(acc.shape[0]):
                acc[i] += times(lhs, rbuf[slot, pl.ds(i * r_tile, r_tile), :])

            @pl.when(step + 2 < chunks)
            def _():
                r_copy(step + 2).start()

            return carry

        lax.fori_loop(0, chunks, reflect_step, 0)

    def down_stage(l, carry):
        @pl.when(lay == l)
        def _():
            down_compute()

        m = jnp.where(l < last, l + 1, last - 1)

        for k in range(2):
            @pl.when((l < layers) & (lay == holder(m, k)))
            def _():
                @pl.when(l < last)
                def _():
                    got_s(k)

                down_sum(l, m, k)

        @pl.when(l == lax.min(lay + 2, layers))
        def _():
            reflect()

        return carry

    lax.fori_loop(0, layers + 1, down_stage, 0)

    def u_copy(k, y):
        p = k * cols + y
        return remote(ubuf.at[p], urec.at[k, col], u_send.at[p], u_recv.at[k, col],
                      (holder(lay, k), row, y))

    def up_compute():
        def lead_step(step, carry):
            b, p = lax.rem(step, ratio), cols + lax.div(step, ratio)
            arrived_g(1, b, p)
            lhs = gup[b, p].reshape(traces, cw)
            j = b * pieces + p
            for i in range(acc.shape[0]):
                acc[i] += times(lhs, tv[j, pl.ds(i * r_tile, r_tile), :])
            return carry

        lax.fori_loop(0, ratio * cols, lead_step, 0)
        for p in range(cols):
            for b in range(ratio):
                arrived_g(1, b, p)

        def piece_step(o, carry):
            k = 1 - lax.div(o, cols)
            y = other(col, cols - 1 - lax.rem(o, cols), cols)
            p = k * cols + y
            for i in range(per):
                tile = p * per + i
                start = pl.multiple_of(tile * r_tile, r_tile)
                total = acc[tile]
                for pp in range(cols):
                    for b in range(ratio):
                        total += times(
                            gup[b, pp].reshape(traces, cw),
                            tv[b * pieces + pp, pl.ds(start, r_tile), :],
                        )
                acc[tile] = total

            @pl.when(o < pieces - 1)
            def _():
                for i in range(per):
                    ubuf[p, :, :, i * r_tile:(i + 1) * r_tile] = (
                        acc[p * per + i].astype(BF16).reshape(cols, part, r_tile)
                    )
                u_copy(k, y).start()

            return carry

        lax.fori_loop(0, pieces, piece_step, 0)

    def o_copy(k, layer, c):
        p = k * cols + col
        return remote(natu.at[k, c], obuf.at[p], o_send.at[k, c], o_recv.at[p], (layer, row, c))

    def up_sum(l, k):
        for d in range(cols):
            if k or d:
                c = other(col, d, cols)
                arrival(urec.at[k, c], u_recv.at[k, c]).wait_recv()
        if k == 0:
            for i in range(per):
                lanes = slice(i * r_tile, (i + 1) * r_tile)
                total = acc[col * per + i].reshape(cols, part, r_tile)
                for d in range(1, cols):
                    total += urec[0, other(col, d, cols), :, :, lanes].astype(F32)
                natu[0, :, :, lanes] = total.astype(BF16)
        else:
            for c in range(cols):
                natu[1, c] = jnp.sum(urec[1, :, c].astype(F32), axis=0).astype(BF16)

        @pl.when(l > 0)
        def _():
            spread(3 + k, natu.at[k], gup, 1, k, l - 1)

        for c in range(cols):
            mine = (k == 0) & (col == c)

            @pl.when(mine)
            def _():
                obuf[k * cols + col] = natu[k, c]

            @pl.when(jnp.logical_not(mine))
            def _():
                o_copy(k, l, c).start()

    def up_stage(i, carry):
        l = last - i

        @pl.when(lay == l)
        def _():
            up_compute()

        for k in range(2):
            @pl.when(lay == holder(l, k))
            def _():
                up_sum(l, k)

        return carry

    lax.fori_loop(0, layers, up_stage, 0)

    for k in range(2):
        for d in range(cols):
            if k or d:
                p = k * cols + other(col, d, cols)
                arrival(obuf.at[p], o_recv.at[p]).wait_recv()
    for p in range(pieces):
        out_ref[:, p * cw:(p + 1) * cw] = obuf[p]

    @pl.when(lay == 0)
    def _():
        for p in range(pieces):
            for d in range(1, cols):
                first_copy(other(col, d, cols), p).wait_send()

    for k in range(2):
        for d in range(cols):
            if k or d:
                y = other(col, d, cols)
                s_copy(k, y).wait_send()
                u_copy(k, y).wait_send()
    for step in range(chunks):
        d_copy(step)[1].wait_send()

    def sums_sent(l, m, k):
        q = jnp.where(l == last, 2, k)
        same = plane(l) == plane(lay)
        for d in range(cols):
            c = other(col, d, cols)
            for b in range(ratio):
                goal, copy = f_copy(q, c, b)
                sent = goal != row
                if d == 0:
                    sent = sent & jnp.logical_not(same)

                @pl.when(sent)
                def _():
                    copy.wait_send()

        @pl.when(l < last)
        def _():
            for c in range(cols):
                @pl.when(jnp.logical_not((k == 0) & (col == c)))
                def _():
                    n_copy(k, m, c).wait_send()

    def stage_sent(l, carry):
        m = jnp.where(l < last, l + 1, last - 1)
        for k in range(2):
            @pl.when(lay == holder(m, k))
            def _():
                sums_sent(l, m, k)

                @pl.when(l == last)
                def _():
                    spread_sent(2, incp.at[2], gup, 1, k, last)

            @pl.when(lay == holder(l, k))
            def _():
                spread_sent(k, incp.at[k], ginc, 0, k, l)

                @pl.when(l > 0)
                def _():
                    spread_sent(3 + k, natu.at[k], gup, 1, k, l - 1)

                for c in range(cols):
                    @pl.when(jnp.logical_not((k == 0) & (col == c)))
                    def _():
                        o_copy(k, l, c).wait_send()

        return carry

    lax.fori_loop(0, layers, stage_sent, 0)


def per_device(layers, rows, cols, sources, transmission, reflection):
    ratio = rows // cols
    own, width = sources.shape[1], sources.shape[2]
    pieces = 2 * cols
    if layers % 2 or layers < 4 or rows % cols or width % (pieces * 128):
        return plain_per_device(layers, rows, cols, sources, transmission, reflection)
    part = -(-own // 16) * 16
    cw = width // pieces
    chunks = ratio * pieces
    r_tile = 256 if cw % 256 == 0 else 128
    traces = cols * part
    src = jnp.pad(sources[0], ((0, part - own), (0, 0)))
    dma, vmem = pltpu.SemaphoreType.DMA, pltpu.VMEM
    result = pl.pallas_call(
        functools.partial(kernel, layers, rows, cols, r_tile),
        out_shape=jax.ShapeDtypeStruct((part, width), BF16),
        in_specs=[
            pl.BlockSpec(memory_space=pltpu.VMEM),
            pl.BlockSpec(memory_space=pl.ANY),
            pl.BlockSpec(memory_space=pl.ANY),
        ],
        out_specs=pl.BlockSpec(memory_space=pltpu.VMEM),
        scratch_shapes=[
            vmem((chunks, width, cw), BF16),
            vmem((2, width, cw), BF16),
            vmem((pieces, part, cw), BF16),
            vmem((2, cols, part, cw), BF16),
            vmem((pieces, cols, part, cw), BF16),
            vmem((chunks, cols, part, cw), BF16),
            vmem((3, cols, ratio, cols, part, cw), BF16),
            vmem((3, rows, cols, part, cw), BF16),
            vmem((3, cols, part, cw), BF16),
            vmem((ratio, pieces, cols, part, cw), BF16),
            vmem((ratio, pieces, cols, part, cw), BF16),
            vmem((width // r_tile, traces, r_tile), F32),
            vmem((pieces, cols, part, cw), BF16),
            vmem((2, cols, cols, part, cw), BF16),
            vmem((2, cols, part, cw), BF16),
            vmem((pieces, part, cw), BF16),
            dma((chunks,)), dma((2,)),
            dma((2, cols)), dma((2, cols)),
            dma((cols, pieces)), dma((cols, pieces)),
            dma((chunks,)), dma((3, cols, ratio)), dma((3, cols, ratio)), dma((3, rows)),
            dma((2, cols)), dma((pieces,)),
            dma((5, rows)), dma((2, ratio, pieces)),
            dma((pieces,)), dma((2, cols)), dma((2, cols)), dma((pieces,)),
        ],
        compiler_params=pltpu.CompilerParams(
            collective_id=0, has_side_effects=True, vmem_limit_bytes=66_000_000
        ),
    )(src, transmission[0], reflection[0])
    return result[None, :own]


def plain_kernel(
    layers, rows, cols, pieces, r_tile,
    src_ref, trans_ref, refl_ref, out_ref,
    tv, rbuf, sall, nin, incn, pbuf, ybuf, zbuf, natd, natu, ginc, gup, acc, ubuf, urec,
    t_sem, r_sem, s_send, s_recv, n_send, n_recv, y_send, y_recv, z_send, z_recv,
    g_send, g_recv, u_send, u_recv, go_sem,
):
    ratio = rows // cols
    chunks = ratio * pieces
    lay, row, col = (lax.axis_index(name) for name in ("layer", "row", "col"))
    part, cw = natd.shape[1], natd.shape[2]
    traces = cols * part
    tiles = acc.shape[0]
    last = layers - 1
    home_col, home_b = lax.div(row, ratio), lax.rem(row, ratio)

    def other(index, by, size):
        return lax.rem(index + by, size)

    def remote(src, dst, send, recv, target):
        return pltpu.make_async_remote_copy(
            src_ref=src, dst_ref=dst, send_sem=send, recv_sem=recv,
            device_id=target, device_id_type=MESH,
        )

    def column_block(step):
        return lax.rem(step, ratio) * pieces + lax.div(step, ratio)

    def t_copy(j):
        start = pl.multiple_of(j * cw, 128)
        return pltpu.make_async_copy(trans_ref.at[:, pl.ds(start, cw)], tv.at[j], t_sem.at[j])

    def r_copy(step):
        start = pl.multiple_of(column_block(step) * cw, 128)
        slot = lax.rem(step, 2)
        return pltpu.make_async_copy(
            refl_ref.at[:, pl.ds(start, cw)], rbuf.at[slot], r_sem.at[slot]
        )

    def copy_src(c):
        return remote(sall.at[col], sall.at[col], s_send.at[c], s_recv.at[col], (lay, row, c))

    def got_src(c):
        return remote(sall.at[c], sall.at[c], s_send.at[c], s_recv.at[c], (lay, row, c))

    def copy_next(c, p):
        return remote(natd.at[p], nin.at[col, p], n_send.at[c, p], n_recv.at[col, p],
                      (lax.min(lay + 1, last), row, c))

    def got_next(c, p):
        return remote(natd.at[p], nin.at[c, p], n_send.at[c, p], n_recv.at[c, p],
                      (lax.max(lay - 1, 0), row, c))

    def copy_y(c, j):
        return remote(pbuf.at[j, c], ybuf.at[col, j], y_send.at[c, j], y_recv.at[col, j],
                      (lay, row, c))

    def got_y(c, j):
        return remote(pbuf.at[j, c], ybuf.at[c, j], y_send.at[c, j], y_recv.at[c, j],
                      (lay, row, c))

    def copy_z(c, j, own):
        block = pbuf.at[j, col] if own else ybuf.at[c, j]
        goal = ratio * c + lax.div(j, pieces)
        return goal, block, remote(
            block, zbuf.at[row, lax.rem(j, pieces)], z_send.at[c, j],
            z_recv.at[row, lax.rem(j, pieces)], (lay, goal, col),
        )

    def got_z(r, p):
        return remote(natd.at[p], zbuf.at[r, p], z_send.at[0, 0], z_recv.at[r, p],
                      (lay, r, col))

    def copy_g(which, p, r):
        block = incn.at[p, col] if which == 0 else (natd, natu)[which - 1].at[p]
        buf, slot = (ginc, 0) if which == 0 else (gup, 1)
        target = lax.max(lay - 1, 0) if which == 2 else lay
        return block, buf, remote(
            block, buf.at[home_b, p, col], g_send.at[which, p, r],
            g_recv.at[slot, p, home_b, col], (target, r, home_col),
        )

    def got_g(slot, p, b, c):
        buf = gup if slot else ginc
        return remote(natd.at[p], buf.at[b, p, c], g_send.at[0, 0, 0],
                      g_recv.at[slot, p, b, c], (lay, ratio * col + b, c))

    def send_g(which, p):
        for d in range(1, rows):
            copy_g(which, p, other(row, d, rows))[2].start()
        block, buf, copy = copy_g(which, p, row)
        if which == 2:
            copy.start()
            return

        @pl.when(home_col == col)
        def _():
            buf[home_b, p, col] = block[...]

        @pl.when(home_col != col)
        def _():
            copy.start()

    def sent_g(which, p):
        for d in range(1, rows):
            copy_g(which, p, other(row, d, rows))[2].wait_send()
        copy = copy_g(which, p, row)[2]
        if which == 2:
            copy.wait_send()
            return

        @pl.when(home_col != col)
        def _():
            copy.wait_send()

    def arrived_g(slot, p, b):
        for c in range(cols):
            mine = (ratio * col + b == row) & (col == c)
            if slot:
                mine = mine & (lay == last)

            @pl.when(jnp.logical_not(mine))
            def _():
                got_g(slot, p, b, c).wait_recv()

    def copy_u(c, p):
        return remote(ubuf.at[c, p], urec.at[col, p], u_send.at[c, p], u_recv.at[col, p],
                      (lay, row, c))

    def got_u(c, p):
        return remote(ubuf.at[c, p], urec.at[c, p], u_send.at[c, p], u_recv.at[c, p],
                      (lay, row, c))

    for step in range(chunks):
        t_copy((step % ratio) * pieces + step // ratio).start()

    barrier = pltpu.get_barrier_semaphore()

    def greet(target):
        pl.semaphore_signal(barrier, inc=1, device_id=target, device_id_type=MESH)

    for dr in range(rows):
        for dc in range(cols):
            if dr or dc:
                greet((lay, other(row, dr, rows), other(col, dc, cols)))

    @pl.when(lay > 0)
    def _():
        for r in range(rows):
            for c in range(cols):
                greet((lay - 1, r, c))

    @pl.when(lay < last)
    def _():
        for r in range(rows):
            for c in range(cols):
                greet((lay + 1, r, c))

    near = (lay > 0).astype(jnp.int32) + (lay < last).astype(jnp.int32)
    pl.semaphore_wait(barrier, rows * cols - 1 + rows * cols * near)

    for p in range(pieces):
        sall[col, p] = src_ref[:, p * cw:(p + 1) * cw]
    for d in range(1, cols):
        copy_src(other(col, d, cols)).start()
    for step in range(2):
        r_copy(step).start()
    acc[...] = jnp.zeros_like(acc)
    for d in range(1, cols):
        got_src(other(col, d, cols)).wait_recv()

    @pl.when(lay == 0)
    def _():
        for p in range(pieces):
            incn[p] = sall[:, p]

    @pl.when(lay > 0)
    def _():
        for p in range(pieces):
            for c in range(cols):
                got_next(c, p).wait_recv()
            incn[p] = (nin[:, p].astype(F32) + sall[:, p].astype(F32)).astype(BF16)

    def to_row(c, j, own):
        goal, block, copy = copy_z(c, j, own)

        @pl.when(goal == row)
        def _():
            zbuf[row, lax.rem(j, pieces)] = block[...]

        @pl.when(goal != row)
        def _():
            copy.start()

    def forward(j):
        for d in range(1, cols):
            c = other(col, d, cols)
            got_y(c, j).wait_recv()
            to_row(c, j, False)

    def down_step(step, carry):
        j = column_block(step)
        t_copy(j).wait()
        total = jnp.zeros((traces, cw), F32)
        for p in range(pieces):
            total += jnp.dot(
                incn[p].reshape(traces, cw), tv[j, pl.ds(p * cw, cw), :],
                preferred_element_type=F32,
            )
        pbuf[j] = total.astype(BF16).reshape(cols, part, cw)
        for d in range(1, cols):
            copy_y(other(col, d, cols), j).start()
        to_row(col, j, True)

        @pl.when(step > 0)
        def _():
            forward(column_block(step - 1))

        return carry

    lax.fori_loop(0, chunks, down_step, 0)
    forward(column_block(chunks - 1))

    @pl.when(lay == last)
    def _():
        for p in range(pieces):
            send_g(0, p)

    for p in range(pieces):
        for d in range(1, rows):
            got_z(other(row, d, rows), p).wait_recv()
        natd[p] = jnp.sum(zbuf[:, p].astype(F32), axis=0).astype(BF16)

        @pl.when(lay < last)
        def _():
            for c in range(cols):
                copy_next(c, p).start()

        @pl.when(lay == last)
        def _():
            send_g(1, p)

    def signal_go():
        pl.semaphore_signal(
            go_sem, inc=1, device_id=(lay - 1, row, col), device_id_type=MESH
        )

    @pl.when((lay > 0) & (lay < last))
    def _():
        signal_go()

    @pl.when(lay < last)
    def _():
        early = pieces // 2
        for p in range(early):
            send_g(0, p)
        pl.semaphore_wait(go_sem, 1)
        for p in range(early, pieces):
            send_g(0, p)

    contract = (((1,), (1,)), ((), ()))

    def times(lhs, rhs):
        return lax.dot_general(lhs, rhs, contract, preferred_element_type=F32)

    def add_product(lhs, weights):
        for i in range(tiles):
            acc[i] += times(lhs, weights[pl.ds(i * r_tile, r_tile), :])

    def reflect_step(step, carry):
        b, p = lax.rem(step, ratio), lax.div(step, ratio)
        arrived_g(0, p, b)
        r_copy(step).wait()
        add_product(ginc[b, p].reshape(traces, cw), rbuf.at[lax.rem(step, 2)])

        @pl.when(step + 2 < chunks)
        def _():
            r_copy(step + 2).start()

        return carry

    lax.fori_loop(0, chunks, reflect_step, 0)

    def up_step(step, carry):
        b, p = lax.rem(step, ratio), lax.div(step, ratio)
        arrived_g(1, p, b)
        add_product(gup[b, p].reshape(traces, cw), tv.at[b * pieces + p])
        return carry

    lax.fori_loop(0, chunks - ratio, up_step, 0)
    end = pieces - 1
    for b in range(ratio):
        arrived_g(1, end, b)

    @pl.when((lay > 0) & (lay == last))
    def _():
        signal_go()

    per = cw // r_tile

    def piece_of(p, c):
        found = []
        for i in range(per):
            found.append(acc[p * per + i, pl.ds(pl.multiple_of(c * part, 8), part), :])
        return jnp.concatenate(found, axis=1)

    for p in range(pieces):
        for i in range(p * per, (p + 1) * per):
            total = acc[i]
            for b in range(ratio):
                total += times(
                    gup[b, end].reshape(traces, cw),
                    tv[b * pieces + end, pl.ds(i * r_tile, r_tile), :],
                )
            acc[i] = total
        for d in range(1, cols):
            c = other(col, d, cols)
            ubuf[c, p] = piece_of(p, c).astype(BF16)
            copy_u(c, p).start()

    for p in range(pieces):
        total = piece_of(p, col)
        for d in range(1, cols):
            c = other(col, d, cols)
            got_u(c, p).wait_recv()
            total += urec[c, p].astype(F32)
        result = total.astype(BF16)
        natu[p] = result
        out_ref[:, p * cw:(p + 1) * cw] = result

        @pl.when(lay > 0)
        def _():
            send_g(2, p)

    for d in range(1, cols):
        c = other(col, d, cols)
        copy_src(c).wait_send()
        for p in range(pieces):
            copy_u(c, p).wait_send()
        for j in range(chunks):
            copy_y(c, j).wait_send()
    for d in range(cols):
        c = other(col, d, cols)
        for j in range(chunks):
            goal, _, copy = copy_z(c, j, d == 0)

            @pl.when(goal != row)
            def _():
                copy.wait_send()

    for p in range(pieces):
        sent_g(0, p)

        @pl.when(lay < last)
        def _():
            for c in range(cols):
                copy_next(c, p).wait_send()

        @pl.when(lay == last)
        def _():
            sent_g(1, p)

        @pl.when(lay > 0)
        def _():
            sent_g(2, p)


def split_of(width):
    for pieces in (4, 3, 2):
        if width % (pieces * 128) == 0:
            return pieces
    return 1


def plain_per_device(layers, rows, cols, sources, transmission, reflection):
    ratio = rows // cols
    own, width = sources.shape[1], sources.shape[2]
    part = -(-own // 16) * 16
    pieces = split_of(width)
    cw = width // pieces
    chunks = ratio * pieces
    r_tile = 256 if cw % 256 == 0 else 128
    traces = cols * part
    src = jnp.pad(sources[0], ((0, part - own), (0, 0)))
    dma, vmem = pltpu.SemaphoreType.DMA, pltpu.VMEM
    result = pl.pallas_call(
        functools.partial(plain_kernel, layers, rows, cols, pieces, r_tile),
        out_shape=jax.ShapeDtypeStruct((part, width), BF16),
        in_specs=[
            pl.BlockSpec(memory_space=pltpu.VMEM),
            pl.BlockSpec(memory_space=pl.ANY),
            pl.BlockSpec(memory_space=pl.ANY),
        ],
        out_specs=pl.BlockSpec(memory_space=pltpu.VMEM),
        scratch_shapes=[
            vmem((chunks, width, cw), BF16),
            vmem((2, width, cw), BF16),
            vmem((cols, pieces, part, cw), BF16),
            vmem((cols, pieces, part, cw), BF16),
            vmem((pieces, cols, part, cw), BF16),
            vmem((chunks, cols, part, cw), BF16),
            vmem((cols, chunks, part, cw), BF16),
            vmem((rows, pieces, part, cw), BF16),
            vmem((pieces, part, cw), BF16),
            vmem((pieces, part, cw), BF16),
            vmem((ratio, pieces, cols, part, cw), BF16),
            vmem((ratio, pieces, cols, part, cw), BF16),
            vmem((width // r_tile, traces, r_tile), F32),
            vmem((cols, pieces, part, cw), BF16),
            vmem((cols, pieces, part, cw), BF16),
            dma((chunks,)), dma((2,)),
            dma((cols,)), dma((cols,)),
            dma((cols, pieces)), dma((cols, pieces)),
            dma((cols, chunks)), dma((cols, chunks)),
            dma((cols, chunks)), dma((rows, pieces)),
            dma((3, pieces, rows)), dma((2, pieces, ratio, cols)),
            dma((cols, pieces)), dma((cols, pieces)),
            pltpu.SemaphoreType.REGULAR,
        ],
        compiler_params=pltpu.CompilerParams(
            collective_id=0, has_side_effects=True, vmem_limit_bytes=66_000_000
        ),
    )(src, transmission[0], reflection[0])
    return result[None, :own]


def solution(mesh):
    sizes = [mesh.shape[name] for name in ("layer", "row", "col")]
    return jax.shard_map(
        functools.partial(per_device, *sizes),
        mesh=mesh,
        in_specs=(P("layer", "col", "row"), P("layer", "row", "col"), P("layer", "row", "col")),
        out_specs=P("layer", "col", "row"),
        check_vma=False,
    )
```

```python
import functools

import jax
import jax.numpy as jnp
from jax import lax
from jax.experimental import pallas as pl
from jax.experimental.pallas import tpu as pltpu
from jax.sharding import PartitionSpec as P

MESH = pl.DeviceIdType.MESH
BF16 = jnp.bfloat16
F32 = jnp.float32


def kernel(
    layers, rows, cols, r_tile,
    src_ref, trans_ref, refl_ref, out_ref,
    tv, rbuf, ssend, sp, incn, pbuf, rel, zbuf, incp, ginc, gup, acc, ubuf, urec, natu, obuf,
    t_sem, r_sem, s_send, s_recv, i_send, i_recv, d_send, rel_recv, f_send, z_recv,
    n_send, n_recv, g_send, g_recv, u_send, u_recv, o_send, o_recv, go_sem,
):
    ratio = rows // cols
    half = layers // 2
    pieces = 2 * cols
    chunks = ratio * pieces
    lay, row, col = (lax.axis_index(name) for name in ("layer", "row", "col"))
    part, cw = pbuf.shape[2], pbuf.shape[3]
    traces = cols * part
    per = cw // r_tile
    last = layers - 1
    late = last - 2
    home_col, home_b = lax.div(row, ratio), lax.rem(row, ratio)

    def other(index, by, size):
        return lax.rem(index + by, size)

    def peer(layer):
        return lax.rem(layer + half, layers)

    def holder(layer, k):
        if isinstance(layer, int):
            return (layer + k * half) % layers
        return lax.rem(layer + k * half, layers)

    def plane(layer):
        return lax.div(layer, half)

    def remote(src, dst, send, recv, target):
        return pltpu.make_async_remote_copy(
            src_ref=src, dst_ref=dst, send_sem=send, recv_sem=recv,
            device_id=target, device_id_type=MESH,
        )

    me = (lay, row, col)
    up_peer = lax.rem(lay + 1, layers)

    def arrival(dst, recv):
        return remote(dst, dst, recv, recv, (up_peer, row, col))

    base = jnp.where(lay < last, lay + 1, last - 1)
    near_k = jnp.where(plane(base) == plane(lay), 0, 1)

    def order(step):
        o, b = lax.div(step, ratio), lax.rem(step, ratio)
        near = lax.div(o, cols)
        d = cols - 1 - lax.rem(o, cols)
        k = jnp.where(near == 1, near_k, 1 - near_k)
        y = other(col, d, cols)
        return near, d, k, y, b, k * cols + y

    def t_copy(j):
        start = pl.multiple_of(j * cw, 128)
        return pltpu.make_async_copy(trans_ref.at[:, pl.ds(start, cw)], tv.at[j], t_sem.at[j])

    def r_index(step):
        p, b = lax.div(step, ratio), lax.rem(step, ratio)
        return b, p

    def r_copy(step):
        b, p = r_index(step)
        start = pl.multiple_of((b * pieces + p) * cw, 128)
        slot = lax.rem(step, 2)
        return pltpu.make_async_copy(
            refl_ref.at[:, pl.ds(start, cw)], rbuf.at[slot], r_sem.at[slot]
        )

    for step in range(chunks):
        b, p = order(step)[-2:]
        t_copy(b * pieces + p).start()

    barrier = pltpu.get_barrier_semaphore()
    for dl in range(layers):
        for dr in range(rows):
            for dc in range(cols):
                if dl or dr or dc:
                    pl.semaphore_signal(
                        barrier, inc=1, device_id_type=MESH,
                        device_id=(other(lay, dl, layers), other(row, dr, rows), other(col, dc, cols)),
                    )
    pl.semaphore_wait(barrier, layers * rows * cols - 1)

    for k in range(2):
        for y in range(cols):
            p = k * cols + y
            ssend[p] = src_ref[:, p * cw:(p + 1) * cw]

    def first_copy(c, p):
        return remote(ssend.at[p], incn.at[p, col], i_send.at[c, p], i_recv.at[col, p], (lay, row, c))

    @pl.when(lay == 0)
    def _():
        for p in range(pieces):
            for d in range(1, cols):
                first_copy(other(col, d, cols), p).start()
            incn[p, col] = ssend[p]

    def s_copy(k, y):
        return remote(ssend.at[k * cols + y], sp.at[k, col], s_send.at[k, y], s_recv.at[k, col],
                      (holder(lay, k), row, y))

    for k in (1, 0):
        for d in range(cols):
            if k or d:
                s_copy(k, other(col, d, cols)).start()
    sp[0, col] = ssend[col]
    acc[...] = jnp.zeros_like(acc)

    def got_s(k):
        for d in range(cols):
            if k or d:
                c = other(col, d, cols)
                arrival(sp.at[k, c], s_recv.at[k, c]).wait_recv()

    def g_copy(slot, block, buf, which, k, layer, r, h):
        p = k * cols + col
        return remote(block.at[h], buf.at[home_b, p, h], g_send.at[slot, r, h],
                      g_recv.at[which, home_b, p, h], (layer, r, home_col))

    def spread_part(slot, block, buf, which, k, layer, h):
        for d in range(1, rows):
            g_copy(slot, block, buf, which, k, layer, other(row, d, rows), h).start()
        mine = (layer == lay) & (home_col == col)

        @pl.when(mine)
        def _():
            buf[home_b, k * cols + col, h] = block[h]

        @pl.when(jnp.logical_not(mine))
        def _():
            g_copy(slot, block, buf, which, k, layer, row, h).start()

    def spread(slot, block, buf, which, k, layer):
        for h in range(cols):
            spread_part(slot, block, buf, which, k, layer, h)

    def spread_sent(slot, block, buf, which, k, layer):
        for h in range(cols):
            for d in range(1, rows):
                g_copy(slot, block, buf, which, k, layer, other(row, d, rows), h).wait_send()

            @pl.when(jnp.logical_not((layer == lay) & (home_col == col)))
            def _():
                g_copy(slot, block, buf, which, k, layer, row, h).wait_send()

    def arrived_g(which, b, p):
        buf = gup if which else ginc
        if which:
            for h in range(cols):
                arrival(buf.at[b, p, h], g_recv.at[which, b, p, h]).wait_recv()
            return
        mine = (ratio * col + b == row) & (p == col)

        @pl.when(jnp.logical_not(mine))
        def _():
            for h in range(cols):
                arrival(buf.at[b, p, h], g_recv.at[which, b, p, h]).wait_recv()

    for k in range(2):
        @pl.when(lay == k * half)
        def _():
            got_s(k)
            incp[k] = sp[k]
            spread(k, incp.at[k], ginc, 0, k, 0)

    def d_copy(step, h):
        near, d, k, y, b, p = order(step)
        j = b * pieces + p
        q = jnp.where(lay == last, 2, k)
        target = holder(base, k)
        direct = (near == 1) & (d == 0)
        return direct, remote(
            pbuf.at[j, h], zbuf.at[q, row, h], d_send.at[j, h], z_recv.at[q, row, h],
            (target, ratio * col + b, col),
        ), remote(
            pbuf.at[j, h], rel.at[q, col, b, h], d_send.at[j, h], rel_recv.at[q, col, b, h],
            (target, row, y),
        )

    def down_compute():
        @pl.when(lay == 0)
        def _():
            for p in range(pieces):
                for d in range(1, cols):
                    c = other(col, d, cols)
                    arrival(incn.at[p, c], i_recv.at[c, p]).wait_recv()

        @pl.when(lay > 0)
        def _():
            for k in range(2):
                for d in range(cols):
                    if k or d:
                        p = k * cols + other(col, d, cols)
                        for h in range(cols):
                            arrival(incn.at[p, h], n_recv.at[p, h]).wait_recv()

            @pl.when(lay != late)
            def _():
                spread(0, incp.at[0], ginc, 0, 0, lay)

        def down_step(step, carry):
            b, p = order(step)[-2:]
            j = b * pieces + p
            t_copy(j).wait()
            total = jnp.zeros((traces, cw), F32)
            for i in range(pieces):
                total += jnp.dot(
                    incn[i].reshape(traces, cw), tv[j, pl.ds(i * cw, cw), :],
                    preferred_element_type=F32,
                )
            pbuf[j] = total.astype(BF16).reshape(cols, part, cw)
            for h in range(cols):
                direct, straight, relayed = d_copy(step, h)

                @pl.when(direct)
                def _():
                    straight.start()

                @pl.when(jnp.logical_not(direct))
                def _():
                    relayed.start()

            return carry

        lax.fori_loop(0, chunks, down_step, 0)
        for step in range(2):
            r_copy(step).start()

        tiles = acc.shape[0]

        def turn_step(step, carry):
            at, i = lax.div(step, tiles), lax.rem(step, tiles)
            j = lax.rem(at, ratio) * pieces + lax.div(at, ratio)
            rows_at = pl.ds(pl.multiple_of(i * r_tile, r_tile), r_tile)
            turned = [tv[j, rows_at, n * r_tile:(n + 1) * r_tile].T for n in range(per)]
            for n in range(per):
                tv[j, rows_at, n * r_tile:(n + 1) * r_tile] = turned[n]
            return carry

        turns = jnp.where(lay == last, cols, pieces) * (ratio * tiles)
        lax.fori_loop(0, turns, turn_step, 0)

    def f_copy(q, c, b, h):
        goal = ratio * c + b
        return goal, remote(rel.at[q, c, b, h], zbuf.at[q, row, h], f_send.at[q, c, b, h],
                            z_recv.at[q, row, h], (lay, goal, col))

    def n_copy(k, layer, c, h):
        p = k * cols + col
        return remote(incp.at[k, h], incn.at[p, h], n_send.at[k, c, h], n_recv.at[p, h],
                      (layer, row, c))

    def forward(q, c):
        for b in range(ratio):
            for h in range(cols):
                arrival(rel.at[q, c, b, h], rel_recv.at[q, c, b, h]).wait_recv()
                goal, copy = f_copy(q, c, b, h)

                @pl.when(goal == row)
                def _():
                    zbuf[q, row, h] = rel[q, c, b, h]

                @pl.when(goal != row)
                def _():
                    copy.start()

    def down_sum(l, m, k):
        q = jnp.where(l == last, 2, k)
        same = plane(l) == plane(lay)
        for d in range(1, cols):
            forward(q, other(col, d, cols))

        @pl.when(jnp.logical_not(same))
        def _():
            forward(q, col)

        for h in range(cols):
            for d in range(rows):
                r = other(row, d, rows)
                if d:
                    arrival(zbuf.at[q, r, h], z_recv.at[q, r, h]).wait_recv()
                else:
                    @pl.when(same & (home_col == col))
                    def _():
                        arrival(zbuf.at[q, r, h], z_recv.at[q, r, h]).wait_recv()

            down = jnp.sum(zbuf[q, :, h].astype(F32), axis=0).astype(BF16)

            @pl.when(l < last)
            def _():
                incp[k, h] = (down.astype(F32) + sp[k, h].astype(F32)).astype(BF16)
                for c in range(cols):
                    mine = (k == 0) & (col == c)

                    @pl.when(mine)
                    def _():
                        incn[k * cols + col, h] = incp[k, h]

                    @pl.when(jnp.logical_not(mine))
                    def _():
                        n_copy(k, m, c, h).start()

            @pl.when(l == last)
            def _():
                incp[2, h] = down
                spread_part(2, incp.at[2], gup, 1, k, last, h)

        if k == 1:
            @pl.when(l < last)
            def _():
                for c in range(cols):
                    for h in range(cols):
                        n_copy(k, m, c, h).wait_send()

                @pl.when(m != late)
                def _():
                    spread(k, incp.at[k], ginc, 0, k, m)

    contract = (((1,), (1,)), ((), ()))

    def times(lhs, rhs):
        return lax.dot_general(lhs, rhs, contract, preferred_element_type=F32)

    def reflect():
        def reflect_step(step, carry):
            b, p = r_index(step)
            arrived_g(0, b, p)
            r_copy(step).wait()
            lhs = ginc[b, p].reshape(traces, cw)
            slot = lax.rem(step, 2)
            for i in range(acc.shape[0]):
                acc[i] += times(lhs, rbuf[slot, pl.ds(i * r_tile, r_tile), :])

            @pl.when(step + 2 < chunks)
            def _():
                r_copy(step + 2).start()

            return carry

        lax.fori_loop(0, chunks, reflect_step, 0)

    def u_copy(k, y, h):
        p = k * cols + y
        return remote(ubuf.at[p, h], urec.at[k, col, h], u_send.at[p, h], u_recv.at[k, col, h],
                      (holder(lay, k), row, y))

    def times_turned(lhs, j, start):
        total = None
        for n in range(per):
            term = jnp.dot(
                lhs[:, n * r_tile:(n + 1) * r_tile],
                tv[j, pl.ds(start, r_tile), n * r_tile:(n + 1) * r_tile],
                preferred_element_type=F32,
            )
            total = term if total is None else total + term
        return total

    def up_compute():
        def lead_step(step, carry):
            b, p = lax.rem(step, ratio), cols + lax.div(step, ratio)
            arrived_g(1, b, p)

            @pl.when((step == 0) & (lay == last))
            def _():
                for k in range(2):
                    target = holder(late, k)
                    if target == last:
                        spread(k, incp.at[k], ginc, 0, k, late)
                    else:
                        pl.semaphore_signal(
                            go_sem, inc=1, device_id=(target, row, col), device_id_type=MESH
                        )

            lhs = gup[b, p].reshape(traces, cw)
            j = b * pieces + p

            @pl.when(lay == last)
            def _():
                for i in range(acc.shape[0]):
                    acc[i] += times(lhs, tv[j, pl.ds(i * r_tile, r_tile), :])

            @pl.when(lay < last)
            def _():
                for i in range(acc.shape[0]):
                    acc[i] += times_turned(lhs, j, i * r_tile)

            return carry

        lax.fori_loop(0, ratio * cols, lead_step, 0)
        for p in range(cols):
            for b in range(ratio):
                arrived_g(1, b, p)

        def piece_step(o, carry):
            k = 1 - lax.div(o, cols)
            y = other(col, cols - 1 - lax.rem(o, cols), cols)
            p = k * cols + y
            for i in range(per):
                tile = p * per + i
                start = pl.multiple_of(tile * r_tile, r_tile)
                total = acc[tile]
                for pp in range(cols):
                    for b in range(ratio):
                        total += times_turned(
                            gup[b, pp].reshape(traces, cw), b * pieces + pp, start
                        )
                acc[tile] = total

            @pl.when(o < pieces - 1)
            def _():
                for i in range(per):
                    ubuf[p, :, :, i * r_tile:(i + 1) * r_tile] = (
                        acc[p * per + i].astype(BF16).reshape(cols, part, r_tile)
                    )
                for h in range(cols):
                    u_copy(k, y, h).start()

            return carry

        lax.fori_loop(0, pieces, piece_step, 0)

    def o_copy(k, layer, c):
        p = k * cols + col
        return remote(natu.at[k, c], obuf.at[p], o_send.at[k, c], o_recv.at[p], (layer, row, c))

    def up_sum(l, k):
        for h in range(cols):
            for d in range(cols):
                if k or d:
                    c = other(col, d, cols)
                    arrival(urec.at[k, c, h], u_recv.at[k, c, h]).wait_recv()
            if k == 0:
                for i in range(per):
                    lanes = slice(i * r_tile, (i + 1) * r_tile)
                    total = acc[col * per + i, h * part:(h + 1) * part]
                    for d in range(1, cols):
                        total += urec[0, other(col, d, cols), h, :, lanes].astype(F32)
                    natu[0, h, :, lanes] = total.astype(BF16)
            else:
                natu[1, h] = jnp.sum(urec[1, :, h].astype(F32), axis=0).astype(BF16)

            @pl.when(l > 0)
            def _():
                spread_part(3 + k, natu.at[k], gup, 1, k, l - 1, h)

        for c in range(cols):
            mine = (k == 0) & (col == c)

            @pl.when(mine)
            def _():
                obuf[k * cols + col] = natu[k, c]

            @pl.when(jnp.logical_not(mine))
            def _():
                o_copy(k, l, c).start()

    def stage(t, carry):
        down = t < layers
        l = jnp.where(down, t, 2 * layers - 1 - t)

        @pl.when(down & (lay == l))
        def _():
            down_compute()

        m = jnp.where(l < last, l + 1, last - 1)
        for k in range(2):
            @pl.when(down & (lay == holder(m, k)))
            def _():
                @pl.when(l < last)
                def _():
                    got_s(k)

                down_sum(l, m, k)

        for k in range(2):
            @pl.when((t == layers) & (lay == holder(late, k)) & (lay != last))
            def _():
                pl.semaphore_wait(go_sem, 1)
                spread(k, incp.at[k], ginc, 0, k, late)

        @pl.when(t == jnp.where(lay == late, layers + 1, lax.min(lay + 2, layers)))
        def _():
            reflect()

        @pl.when(jnp.logical_not(down) & (lay == l))
        def _():
            up_compute()

        for k in range(2):
            @pl.when(jnp.logical_not(down) & (lay == holder(l, k)))
            def _():
                up_sum(l, k)

        return carry

    lax.fori_loop(0, 2 * layers, stage, 0)

    for k in range(2):
        for d in range(cols):
            if k or d:
                p = k * cols + other(col, d, cols)
                arrival(obuf.at[p], o_recv.at[p]).wait_recv()
    for p in range(pieces):
        out_ref[:, p * cw:(p + 1) * cw] = obuf[p]

    @pl.when(lay == 0)
    def _():
        for p in range(pieces):
            for d in range(1, cols):
                first_copy(other(col, d, cols), p).wait_send()

    for k in range(2):
        for d in range(cols):
            if k or d:
                y = other(col, d, cols)
                s_copy(k, y).wait_send()
                for h in range(cols):
                    u_copy(k, y, h).wait_send()
    for step in range(chunks):
        for h in range(cols):
            d_copy(step, h)[1].wait_send()

    def sums_sent(l, m, k):
        q = jnp.where(l == last, 2, k)
        same = plane(l) == plane(lay)
        for d in range(cols):
            c = other(col, d, cols)
            for b in range(ratio):
                for h in range(cols):
                    goal, copy = f_copy(q, c, b, h)
                    sent = goal != row
                    if d == 0:
                        sent = sent & jnp.logical_not(same)

                    @pl.when(sent)
                    def _():
                        copy.wait_send()

        if k == 0:
            @pl.when(l < last)
            def _():
                for d in range(1, cols):
                    for h in range(cols):
                        n_copy(k, m, other(col, d, cols), h).wait_send()

    def stage_sent(l, carry):
        m = jnp.where(l < last, l + 1, last - 1)
        for k in range(2):
            @pl.when(lay == holder(m, k))
            def _():
                sums_sent(l, m, k)

                @pl.when(l == last)
                def _():
                    spread_sent(2, incp.at[2], gup, 1, k, last)

            @pl.when(lay == holder(l, k))
            def _():
                spread_sent(k, incp.at[k], ginc, 0, k, l)

                @pl.when(l > 0)
                def _():
                    spread_sent(3 + k, natu.at[k], gup, 1, k, l - 1)

                for c in range(cols):
                    @pl.when(jnp.logical_not((k == 0) & (col == c)))
                    def _():
                        o_copy(k, l, c).wait_send()

        return carry

    lax.fori_loop(0, layers, stage_sent, 0)


def per_device(layers, rows, cols, sources, transmission, reflection):
    ratio = rows // cols
    own, width = sources.shape[1], sources.shape[2]
    pieces = 2 * cols
    if layers % 2 or layers < 4 or rows % cols or width % (pieces * 128):
        return plain_per_device(layers, rows, cols, sources, transmission, reflection)
    part = -(-own // 16) * 16
    cw = width // pieces
    chunks = ratio * pieces
    r_tile = 256 if cw % 256 == 0 else 128
    traces = cols * part
    src = jnp.pad(sources[0], ((0, part - own), (0, 0)))
    dma, vmem = pltpu.SemaphoreType.DMA, pltpu.VMEM
    result = pl.pallas_call(
        functools.partial(kernel, layers, rows, cols, r_tile),
        out_shape=jax.ShapeDtypeStruct((part, width), BF16),
        in_specs=[
            pl.BlockSpec(memory_space=pltpu.VMEM),
            pl.BlockSpec(memory_space=pl.ANY),
            pl.BlockSpec(memory_space=pl.ANY),
        ],
        out_specs=pl.BlockSpec(memory_space=pltpu.VMEM),
        scratch_shapes=[
            vmem((chunks, width, cw), BF16),
            vmem((2, width, cw), BF16),
            vmem((pieces, part, cw), BF16),
            vmem((2, cols, part, cw), BF16),
            vmem((pieces, cols, part, cw), BF16),
            vmem((chunks, cols, part, cw), BF16),
            vmem((3, cols, ratio, cols, part, cw), BF16),
            vmem((3, rows, cols, part, cw), BF16),
            vmem((3, cols, part, cw), BF16),
            vmem((ratio, pieces, cols, part, cw), BF16),
            vmem((ratio, pieces, cols, part, cw), BF16),
            vmem((width // r_tile, traces, r_tile), F32),
            vmem((pieces, cols, part, cw), BF16),
            vmem((2, cols, cols, part, cw), BF16),
            vmem((2, cols, part, cw), BF16),
            vmem((pieces, part, cw), BF16),
            dma((chunks,)), dma((2,)),
            dma((2, cols)), dma((2, cols)),
            dma((cols, pieces)), dma((cols, pieces)),
            dma((chunks, cols)), dma((3, cols, ratio, cols)),
            dma((3, cols, ratio, cols)), dma((3, rows, cols)),
            dma((2, cols, cols)), dma((pieces, cols)),
            dma((5, rows, cols)), dma((2, ratio, pieces, cols)),
            dma((pieces, cols)), dma((2, cols, cols)), dma((2, cols)), dma((pieces,)),
            pltpu.SemaphoreType.REGULAR,
        ],
        compiler_params=pltpu.CompilerParams(
            collective_id=0, has_side_effects=True, vmem_limit_bytes=66_000_000
        ),
    )(src, transmission[0], reflection[0])
    return result[None, :own]


def plain_kernel(
    layers, rows, cols, pieces, r_tile,
    src_ref, trans_ref, refl_ref, out_ref,
    tv, rbuf, sall, nin, incn, pbuf, ybuf, zbuf, natd, natu, ginc, gup, acc, ubuf, urec,
    t_sem, r_sem, s_send, s_recv, n_send, n_recv, y_send, y_recv, z_send, z_recv,
    g_send, g_recv, u_send, u_recv, go_sem,
):
    ratio = rows // cols
    chunks = ratio * pieces
    lay, row, col = (lax.axis_index(name) for name in ("layer", "row", "col"))
    part, cw = natd.shape[1], natd.shape[2]
    traces = cols * part
    tiles = acc.shape[0]
    last = layers - 1
    home_col, home_b = lax.div(row, ratio), lax.rem(row, ratio)

    def other(index, by, size):
        return lax.rem(index + by, size)

    def remote(src, dst, send, recv, target):
        return pltpu.make_async_remote_copy(
            src_ref=src, dst_ref=dst, send_sem=send, recv_sem=recv,
            device_id=target, device_id_type=MESH,
        )

    def column_block(step):
        return lax.rem(step, ratio) * pieces + lax.div(step, ratio)

    def t_copy(j):
        start = pl.multiple_of(j * cw, 128)
        return pltpu.make_async_copy(trans_ref.at[:, pl.ds(start, cw)], tv.at[j], t_sem.at[j])

    def r_copy(step):
        start = pl.multiple_of(column_block(step) * cw, 128)
        slot = lax.rem(step, 2)
        return pltpu.make_async_copy(
            refl_ref.at[:, pl.ds(start, cw)], rbuf.at[slot], r_sem.at[slot]
        )

    def copy_src(c):
        return remote(sall.at[col], sall.at[col], s_send.at[c], s_recv.at[col], (lay, row, c))

    def got_src(c):
        return remote(sall.at[c], sall.at[c], s_send.at[c], s_recv.at[c], (lay, row, c))

    def copy_next(c, p):
        return remote(natd.at[p], nin.at[col, p], n_send.at[c, p], n_recv.at[col, p],
                      (lax.min(lay + 1, last), row, c))

    def got_next(c, p):
        return remote(natd.at[p], nin.at[c, p], n_send.at[c, p], n_recv.at[c, p],
                      (lax.max(lay - 1, 0), row, c))

    def copy_y(c, j):
        return remote(pbuf.at[j, c], ybuf.at[col, j], y_send.at[c, j], y_recv.at[col, j],
                      (lay, row, c))

    def got_y(c, j):
        return remote(pbuf.at[j, c], ybuf.at[c, j], y_send.at[c, j], y_recv.at[c, j],
                      (lay, row, c))

    def copy_z(c, j, own):
        block = pbuf.at[j, col] if own else ybuf.at[c, j]
        goal = ratio * c + lax.div(j, pieces)
        return goal, block, remote(
            block, zbuf.at[row, lax.rem(j, pieces)], z_send.at[c, j],
            z_recv.at[row, lax.rem(j, pieces)], (lay, goal, col),
        )

    def got_z(r, p):
        return remote(natd.at[p], zbuf.at[r, p], z_send.at[0, 0], z_recv.at[r, p],
                      (lay, r, col))

    def copy_g(which, p, r):
        block = incn.at[p, col] if which == 0 else (natd, natu)[which - 1].at[p]
        buf, slot = (ginc, 0) if which == 0 else (gup, 1)
        target = lax.max(lay - 1, 0) if which == 2 else lay
        return block, buf, remote(
            block, buf.at[home_b, p, col], g_send.at[which, p, r],
            g_recv.at[slot, p, home_b, col], (target, r, home_col),
        )

    def got_g(slot, p, b, c):
        buf = gup if slot else ginc
        return remote(natd.at[p], buf.at[b, p, c], g_send.at[0, 0, 0],
                      g_recv.at[slot, p, b, c], (lay, ratio * col + b, c))

    def send_g(which, p):
        for d in range(1, rows):
            copy_g(which, p, other(row, d, rows))[2].start()
        block, buf, copy = copy_g(which, p, row)
        if which == 2:
            copy.start()
            return

        @pl.when(home_col == col)
        def _():
            buf[home_b, p, col] = block[...]

        @pl.when(home_col != col)
        def _():
            copy.start()

    def sent_g(which, p):
        for d in range(1, rows):
            copy_g(which, p, other(row, d, rows))[2].wait_send()
        copy = copy_g(which, p, row)[2]
        if which == 2:
            copy.wait_send()
            return

        @pl.when(home_col != col)
        def _():
            copy.wait_send()

    def arrived_g(slot, p, b):
        for c in range(cols):
            mine = (ratio * col + b == row) & (col == c)
            if slot:
                mine = mine & (lay == last)

            @pl.when(jnp.logical_not(mine))
            def _():
                got_g(slot, p, b, c).wait_recv()

    def copy_u(c, p):
        return remote(ubuf.at[c, p], urec.at[col, p], u_send.at[c, p], u_recv.at[col, p],
                      (lay, row, c))

    def got_u(c, p):
        return remote(ubuf.at[c, p], urec.at[c, p], u_send.at[c, p], u_recv.at[c, p],
                      (lay, row, c))

    for step in range(chunks):
        t_copy((step % ratio) * pieces + step // ratio).start()

    barrier = pltpu.get_barrier_semaphore()

    def greet(target):
        pl.semaphore_signal(barrier, inc=1, device_id=target, device_id_type=MESH)

    for dr in range(rows):
        for dc in range(cols):
            if dr or dc:
                greet((lay, other(row, dr, rows), other(col, dc, cols)))

    @pl.when(lay > 0)
    def _():
        for r in range(rows):
            for c in range(cols):
                greet((lay - 1, r, c))

    @pl.when(lay < last)
    def _():
        for r in range(rows):
            for c in range(cols):
                greet((lay + 1, r, c))

    near = (lay > 0).astype(jnp.int32) + (lay < last).astype(jnp.int32)
    pl.semaphore_wait(barrier, rows * cols - 1 + rows * cols * near)

    for p in range(pieces):
        sall[col, p] = src_ref[:, p * cw:(p + 1) * cw]
    for d in range(1, cols):
        copy_src(other(col, d, cols)).start()
    for step in range(2):
        r_copy(step).start()
    acc[...] = jnp.zeros_like(acc)
    for d in range(1, cols):
        got_src(other(col, d, cols)).wait_recv()

    @pl.when(lay == 0)
    def _():
        for p in range(pieces):
            incn[p] = sall[:, p]

    @pl.when(lay > 0)
    def _():
        for p in range(pieces):
            for c in range(cols):
                got_next(c, p).wait_recv()
            incn[p] = (nin[:, p].astype(F32) + sall[:, p].astype(F32)).astype(BF16)

    def to_row(c, j, own):
        goal, block, copy = copy_z(c, j, own)

        @pl.when(goal == row)
        def _():
            zbuf[row, lax.rem(j, pieces)] = block[...]

        @pl.when(goal != row)
        def _():
            copy.start()

    def forward(j):
        for d in range(1, cols):
            c = other(col, d, cols)
            got_y(c, j).wait_recv()
            to_row(c, j, False)

    def down_step(step, carry):
        j = column_block(step)
        t_copy(j).wait()
        total = jnp.zeros((traces, cw), F32)
        for p in range(pieces):
            total += jnp.dot(
                incn[p].reshape(traces, cw), tv[j, pl.ds(p * cw, cw), :],
                preferred_element_type=F32,
            )
        pbuf[j] = total.astype(BF16).reshape(cols, part, cw)
        for d in range(1, cols):
            copy_y(other(col, d, cols), j).start()
        to_row(col, j, True)

        @pl.when(step > 0)
        def _():
            forward(column_block(step - 1))

        return carry

    lax.fori_loop(0, chunks, down_step, 0)
    forward(column_block(chunks - 1))

    @pl.when(lay == last)
    def _():
        for p in range(pieces):
            send_g(0, p)

    for p in range(pieces):
        for d in range(1, rows):
            got_z(other(row, d, rows), p).wait_recv()
        natd[p] = jnp.sum(zbuf[:, p].astype(F32), axis=0).astype(BF16)

        @pl.when(lay < last)
        def _():
            for c in range(cols):
                copy_next(c, p).start()

        @pl.when(lay == last)
        def _():
            send_g(1, p)

    def signal_go():
        pl.semaphore_signal(
            go_sem, inc=1, device_id=(lay - 1, row, col), device_id_type=MESH
        )

    @pl.when((lay > 0) & (lay < last))
    def _():
        signal_go()

    @pl.when(lay < last)
    def _():
        early = pieces // 2
        for p in range(early):
            send_g(0, p)
        pl.semaphore_wait(go_sem, 1)
        for p in range(early, pieces):
            send_g(0, p)

    contract = (((1,), (1,)), ((), ()))

    def times(lhs, rhs):
        return lax.dot_general(lhs, rhs, contract, preferred_element_type=F32)

    def add_product(lhs, weights):
        for i in range(tiles):
            acc[i] += times(lhs, weights[pl.ds(i * r_tile, r_tile), :])

    def reflect_step(step, carry):
        b, p = lax.rem(step, ratio), lax.div(step, ratio)
        arrived_g(0, p, b)
        r_copy(step).wait()
        add_product(ginc[b, p].reshape(traces, cw), rbuf.at[lax.rem(step, 2)])

        @pl.when(step + 2 < chunks)
        def _():
            r_copy(step + 2).start()

        return carry

    lax.fori_loop(0, chunks, reflect_step, 0)

    def up_step(step, carry):
        b, p = lax.rem(step, ratio), lax.div(step, ratio)
        arrived_g(1, p, b)
        add_product(gup[b, p].reshape(traces, cw), tv.at[b * pieces + p])
        return carry

    lax.fori_loop(0, chunks - ratio, up_step, 0)
    end = pieces - 1
    for b in range(ratio):
        arrived_g(1, end, b)

    @pl.when((lay > 0) & (lay == last))
    def _():
        signal_go()

    per = cw // r_tile

    def piece_of(p, c):
        found = []
        for i in range(per):
            found.append(acc[p * per + i, pl.ds(pl.multiple_of(c * part, 8), part), :])
        return jnp.concatenate(found, axis=1)

    for p in range(pieces):
        for i in range(p * per, (p + 1) * per):
            total = acc[i]
            for b in range(ratio):
                total += times(
                    gup[b, end].reshape(traces, cw),
                    tv[b * pieces + end, pl.ds(i * r_tile, r_tile), :],
                )
            acc[i] = total
        for d in range(1, cols):
            c = other(col, d, cols)
            ubuf[c, p] = piece_of(p, c).astype(BF16)
            copy_u(c, p).start()

    for p in range(pieces):
        total = piece_of(p, col)
        for d in range(1, cols):
            c = other(col, d, cols)
            got_u(c, p).wait_recv()
            total += urec[c, p].astype(F32)
        result = total.astype(BF16)
        natu[p] = result
        out_ref[:, p * cw:(p + 1) * cw] = result

        @pl.when(lay > 0)
        def _():
            send_g(2, p)

    for d in range(1, cols):
        c = other(col, d, cols)
        copy_src(c).wait_send()
        for p in range(pieces):
            copy_u(c, p).wait_send()
        for j in range(chunks):
            copy_y(c, j).wait_send()
    for d in range(cols):
        c = other(col, d, cols)
        for j in range(chunks):
            goal, _, copy = copy_z(c, j, d == 0)

            @pl.when(goal != row)
            def _():
                copy.wait_send()

    for p in range(pieces):
        sent_g(0, p)

        @pl.when(lay < last)
        def _():
            for c in range(cols):
                copy_next(c, p).wait_send()

        @pl.when(lay == last)
        def _():
            sent_g(1, p)

        @pl.when(lay > 0)
        def _():
            sent_g(2, p)


def split_of(width):
    for pieces in (4, 3, 2):
        if width % (pieces * 128) == 0:
            return pieces
    return 1


def plain_per_device(layers, rows, cols, sources, transmission, reflection):
    ratio = rows // cols
    own, width = sources.shape[1], sources.shape[2]
    part = -(-own // 16) * 16
    pieces = split_of(width)
    cw = width // pieces
    chunks = ratio * pieces
    r_tile = 256 if cw % 256 == 0 else 128
    traces = cols * part
    src = jnp.pad(sources[0], ((0, part - own), (0, 0)))
    dma, vmem = pltpu.SemaphoreType.DMA, pltpu.VMEM
    result = pl.pallas_call(
        functools.partial(plain_kernel, layers, rows, cols, pieces, r_tile),
        out_shape=jax.ShapeDtypeStruct((part, width), BF16),
        in_specs=[
            pl.BlockSpec(memory_space=pltpu.VMEM),
            pl.BlockSpec(memory_space=pl.ANY),
            pl.BlockSpec(memory_space=pl.ANY),
        ],
        out_specs=pl.BlockSpec(memory_space=pltpu.VMEM),
        scratch_shapes=[
            vmem((chunks, width, cw), BF16),
            vmem((2, width, cw), BF16),
            vmem((cols, pieces, part, cw), BF16),
            vmem((cols, pieces, part, cw), BF16),
            vmem((pieces, cols, part, cw), BF16),
            vmem((chunks, cols, part, cw), BF16),
            vmem((cols, chunks, part, cw), BF16),
            vmem((rows, pieces, part, cw), BF16),
            vmem((pieces, part, cw), BF16),
            vmem((pieces, part, cw), BF16),
            vmem((ratio, pieces, cols, part, cw), BF16),
            vmem((ratio, pieces, cols, part, cw), BF16),
            vmem((width // r_tile, traces, r_tile), F32),
            vmem((cols, pieces, part, cw), BF16),
            vmem((cols, pieces, part, cw), BF16),
            dma((chunks,)), dma((2,)),
            dma((cols,)), dma((cols,)),
            dma((cols, pieces)), dma((cols, pieces)),
            dma((cols, chunks)), dma((cols, chunks)),
            dma((cols, chunks)), dma((rows, pieces)),
            dma((3, pieces, rows)), dma((2, pieces, ratio, cols)),
            dma((cols, pieces)), dma((cols, pieces)),
            pltpu.SemaphoreType.REGULAR,
        ],
        compiler_params=pltpu.CompilerParams(
            collective_id=0, has_side_effects=True, vmem_limit_bytes=66_000_000
        ),
    )(src, transmission[0], reflection[0])
    return result[None, :own]


def solution(mesh):
    sizes = [mesh.shape[name] for name in ("layer", "row", "col")]
    return jax.shard_map(
        functools.partial(per_device, *sizes),
        mesh=mesh,
        in_specs=(P("layer", "col", "row"), P("layer", "row", "col"), P("layer", "row", "col")),
        out_specs=P("layer", "col", "row"),
        check_vma=False,
    )
```

```python
import functools

import jax
import jax.numpy as jnp
from jax import lax
from jax.experimental import pallas as pl
from jax.experimental.pallas import tpu as pltpu
from jax.sharding import PartitionSpec as P

MESH = pl.DeviceIdType.MESH
BF16 = jnp.bfloat16
F32 = jnp.float32


def kernel(
    layers, rows, cols, r_tile,
    src_ref, trans_ref, refl_ref, out_ref,
    tv, rbuf, ssend, sp, incn, pbuf, rel, zbuf, incp, ginc, gup, acc, ubuf, urec, natu, obuf, vrec,
    t_sem, r_sem, s_send, s_recv, i_send, i_recv, d_send, rel_recv, f_send, z_recv,
    n_send, n_recv, g_send, g_recv, u_send, u_recv, o_send, o_recv, v_send, v_recv, go_sem,
):
    ratio = rows // cols
    half = layers // 2
    pieces = 2 * cols
    chunks = ratio * pieces
    lay, row, col = (lax.axis_index(name) for name in ("layer", "row", "col"))
    part, cw = pbuf.shape[2], pbuf.shape[3]
    traces = cols * part
    per = cw // r_tile
    last = layers - 1
    late = last - 2
    home_col, home_b = lax.div(row, ratio), lax.rem(row, ratio)

    def other(index, by, size):
        return lax.rem(index + by, size)

    def peer(layer):
        return lax.rem(layer + half, layers)

    def holder(layer, k):
        if isinstance(layer, int):
            return (layer + k * half) % layers
        return lax.rem(layer + k * half, layers)

    def plane(layer):
        return lax.div(layer, half)

    def remote(src, dst, send, recv, target):
        return pltpu.make_async_remote_copy(
            src_ref=src, dst_ref=dst, send_sem=send, recv_sem=recv,
            device_id=target, device_id_type=MESH,
        )

    me = (lay, row, col)
    up_peer = lax.rem(lay + 1, layers)

    def arrival(dst, recv):
        return remote(dst, dst, recv, recv, (up_peer, row, col))

    base = jnp.where(lay < last, lay + 1, last - 1)
    near_k = jnp.where(plane(base) == plane(lay), 0, 1)

    def order(step):
        o, b = lax.div(step, ratio), lax.rem(step, ratio)
        near = lax.div(o, cols)
        d = cols - 1 - lax.rem(o, cols)
        k = jnp.where(near == 1, near_k, 1 - near_k)
        y = other(col, d, cols)
        return near, d, k, y, b, k * cols + y

    def t_copy(j):
        start = pl.multiple_of(j * cw, 128)
        return pltpu.make_async_copy(trans_ref.at[:, pl.ds(start, cw)], tv.at[j], t_sem.at[j])

    def r_index(step):
        p, b = lax.div(step, ratio), lax.rem(step, ratio)
        return b, p

    def r_copy(step):
        b, p = r_index(step)
        start = pl.multiple_of((b * pieces + p) * cw, 128)
        slot = lax.rem(step, 2)
        return pltpu.make_async_copy(
            refl_ref.at[:, pl.ds(start, cw)], rbuf.at[slot], r_sem.at[slot]
        )

    for step in range(chunks):
        b, p = order(step)[-2:]
        t_copy(b * pieces + p).start()

    barrier = pltpu.get_barrier_semaphore()
    for dl in range(layers):
        for dr in range(rows):
            for dc in range(cols):
                if dl or dr or dc:
                    pl.semaphore_signal(
                        barrier, inc=1, device_id_type=MESH,
                        device_id=(other(lay, dl, layers), other(row, dr, rows), other(col, dc, cols)),
                    )
    pl.semaphore_wait(barrier, layers * rows * cols - 1)

    for k in range(2):
        for y in range(cols):
            p = k * cols + y
            ssend[p] = src_ref[:, p * cw:(p + 1) * cw]

    def first_copy(c, p):
        return remote(ssend.at[p], incn.at[p, col], i_send.at[c, p], i_recv.at[col, p], (lay, row, c))

    @pl.when(lay == 0)
    def _():
        for p in range(pieces):
            for d in range(1, cols):
                first_copy(other(col, d, cols), p).start()
            incn[p, col] = ssend[p]

    def s_copy(k, y):
        return remote(ssend.at[k * cols + y], sp.at[k, col], s_send.at[k, y], s_recv.at[k, col],
                      (holder(lay, k), row, y))

    for k in (1, 0):
        for d in range(cols):
            if k or d:
                s_copy(k, other(col, d, cols)).start()
    sp[0, col] = ssend[col]
    acc[...] = jnp.zeros_like(acc)

    def got_s(k):
        for d in range(cols):
            if k or d:
                c = other(col, d, cols)
                arrival(sp.at[k, c], s_recv.at[k, c]).wait_recv()

    def g_copy(slot, block, buf, which, k, layer, r, h):
        p = k * cols + col
        return remote(block.at[h], buf.at[home_b, p, h], g_send.at[slot, r, h],
                      g_recv.at[which, home_b, p, h], (layer, r, home_col))

    def spread_part(slot, block, buf, which, k, layer, h):
        for d in range(1, rows):
            g_copy(slot, block, buf, which, k, layer, other(row, d, rows), h).start()
        mine = (layer == lay) & (home_col == col)

        @pl.when(mine)
        def _():
            buf[home_b, k * cols + col, h] = block[h]

        @pl.when(jnp.logical_not(mine))
        def _():
            g_copy(slot, block, buf, which, k, layer, row, h).start()

    def spread(slot, block, buf, which, k, layer):
        for h in range(cols):
            spread_part(slot, block, buf, which, k, layer, h)

    def spread_sent(slot, block, buf, which, k, layer):
        for h in range(cols):
            for d in range(1, rows):
                g_copy(slot, block, buf, which, k, layer, other(row, d, rows), h).wait_send()

            @pl.when(jnp.logical_not((layer == lay) & (home_col == col)))
            def _():
                g_copy(slot, block, buf, which, k, layer, row, h).wait_send()

    def arrived_g(which, b, p):
        buf = gup if which else ginc
        if which:
            for h in range(cols):
                arrival(buf.at[b, p, h], g_recv.at[which, b, p, h]).wait_recv()
            return
        mine = (ratio * col + b == row) & (p == col)

        @pl.when(jnp.logical_not(mine))
        def _():
            for h in range(cols):
                arrival(buf.at[b, p, h], g_recv.at[which, b, p, h]).wait_recv()

    for k in range(2):
        @pl.when(lay == k * half)
        def _():
            got_s(k)
            incp[k] = sp[k]
            if k:
                spread(k, incp.at[k], ginc, 0, k, 0)

    def d_copy(step, h):
        near, d, k, y, b, p = order(step)
        j = b * pieces + p
        q = jnp.where(lay == last, 2, k)
        target = holder(base, k)
        direct = (near == 1) & (d == 0)
        return direct, remote(
            pbuf.at[j, h], zbuf.at[q, row, h], d_send.at[j, h], z_recv.at[q, row, h],
            (target, ratio * col + b, col),
        ), remote(
            pbuf.at[j, h], rel.at[q, col, b, h], d_send.at[j, h], rel_recv.at[q, col, b, h],
            (target, row, y),
        )

    def down_compute():
        @pl.when(lay == 0)
        def _():
            for p in range(pieces):
                for d in range(1, cols):
                    c = other(col, d, cols)
                    arrival(incn.at[p, c], i_recv.at[c, p]).wait_recv()
            spread(0, incp.at[0], ginc, 0, 0, 0)

        @pl.when(lay > 0)
        def _():
            for k in range(2):
                for d in range(cols):
                    if k or d:
                        p = k * cols + other(col, d, cols)
                        for h in range(cols):
                            arrival(incn.at[p, h], n_recv.at[p, h]).wait_recv()

            @pl.when(lay != late)
            def _():
                spread(0, incp.at[0], ginc, 0, 0, lay)

        def down_step(step, carry):
            b, p = order(step)[-2:]
            j = b * pieces + p
            t_copy(j).wait()
            total = jnp.zeros((traces, cw), F32)
            for i in range(pieces):
                total += jnp.dot(
                    incn[i].reshape(traces, cw), tv[j, pl.ds(i * cw, cw), :],
                    preferred_element_type=F32,
                )
            pbuf[j] = total.astype(BF16).reshape(cols, part, cw)
            for h in range(cols):
                direct, straight, relayed = d_copy(step, h)

                @pl.when(direct)
                def _():
                    straight.start()

                @pl.when(jnp.logical_not(direct))
                def _():
                    relayed.start()

            return carry

        lax.fori_loop(0, chunks, down_step, 0)
        for step in range(2):
            r_copy(step).start()

        tiles = acc.shape[0]

        def turn_step(step, carry):
            at, i = lax.div(step, tiles), lax.rem(step, tiles)
            j = lax.rem(at, ratio) * pieces + lax.div(at, ratio)
            rows_at = pl.ds(pl.multiple_of(i * r_tile, r_tile), r_tile)
            turned = [tv[j, rows_at, n * r_tile:(n + 1) * r_tile].T for n in range(per)]
            for n in range(per):
                tv[j, rows_at, n * r_tile:(n + 1) * r_tile] = turned[n]
            return carry

        turns = jnp.where(lay == last, cols, pieces) * (ratio * tiles)
        lax.fori_loop(0, turns, turn_step, 0)

    def f_copy(q, c, b, h):
        goal = ratio * c + b
        return goal, remote(rel.at[q, c, b, h], zbuf.at[q, row, h], f_send.at[q, c, b, h],
                            z_recv.at[q, row, h], (lay, goal, col))

    def n_copy(k, layer, c, h):
        p = k * cols + col
        return remote(incp.at[k, h], incn.at[p, h], n_send.at[k, c, h], n_recv.at[p, h],
                      (layer, row, c))

    def forward(q, c):
        for b in range(ratio):
            for h in range(cols):
                arrival(rel.at[q, c, b, h], rel_recv.at[q, c, b, h]).wait_recv()
                goal, copy = f_copy(q, c, b, h)

                @pl.when(goal == row)
                def _():
                    zbuf[q, row, h] = rel[q, c, b, h]

                @pl.when(goal != row)
                def _():
                    copy.start()

    def down_sum(l, m, k):
        q = jnp.where(l == last, 2, k)
        same = plane(l) == plane(lay)
        for d in range(1, cols):
            forward(q, other(col, d, cols))

        @pl.when(jnp.logical_not(same))
        def _():
            forward(q, col)

        for h in range(cols):
            for d in range(rows):
                r = other(row, d, rows)
                if d:
                    arrival(zbuf.at[q, r, h], z_recv.at[q, r, h]).wait_recv()
                else:
                    @pl.when(same & (home_col == col))
                    def _():
                        arrival(zbuf.at[q, r, h], z_recv.at[q, r, h]).wait_recv()

            down = jnp.sum(zbuf[q, :, h].astype(F32), axis=0).astype(BF16)

            @pl.when(l < last)
            def _():
                incp[k, h] = (down.astype(F32) + sp[k, h].astype(F32)).astype(BF16)
                for d in range(1, cols):
                    n_copy(k, m, other(col, d, cols), h).start()
                if k:
                    n_copy(k, m, col, h).start()
                else:
                    incn[col, h] = incp[k, h]

            @pl.when(l == last)
            def _():
                incp[2, h] = down
                spread_part(2, incp.at[2], gup, 1, k, last, h)

        if k == 1:
            @pl.when(l < last)
            def _():
                for c in range(cols):
                    for h in range(cols):
                        n_copy(k, m, c, h).wait_send()

                @pl.when(m != late)
                def _():
                    spread(k, incp.at[k], ginc, 0, k, m)

    contract = (((1,), (1,)), ((), ()))

    def times(lhs, rhs):
        return lax.dot_general(lhs, rhs, contract, preferred_element_type=F32)

    def reflect():
        def reflect_step(step, carry):
            b, p = r_index(step)
            arrived_g(0, b, p)
            r_copy(step).wait()
            lhs = ginc[b, p].reshape(traces, cw)
            slot = lax.rem(step, 2)
            for i in range(acc.shape[0]):
                acc[i] += times(lhs, rbuf[slot, pl.ds(i * r_tile, r_tile), :])

            @pl.when(step + 2 < chunks)
            def _():
                r_copy(step + 2).start()

            return carry

        lax.fori_loop(0, chunks, reflect_step, 0)

    def u_copy(k, y, h):
        p = k * cols + y
        return remote(ubuf.at[p, h], urec.at[k, col, h], u_send.at[p, h], u_recv.at[k, col, h],
                      (holder(lay, k), row, y))

    def times_turned(lhs, j, start):
        total = None
        for n in range(per):
            term = jnp.dot(
                lhs[:, n * r_tile:(n + 1) * r_tile],
                tv[j, pl.ds(start, r_tile), n * r_tile:(n + 1) * r_tile],
                preferred_element_type=F32,
            )
            total = term if total is None else total + term
        return total

    def v_copy(c, p):
        return remote(ubuf.at[p, c], vrec.at[col, p], v_send.at[c, p], v_recv.at[col, p],
                      (lay, row, c))

    def top_sum():
        mine = pl.ds(pl.multiple_of(col * part, 16), part)
        for p in list(range(cols, pieces)) + list(range(cols)):
            for d in range(1, cols):
                c = other(col, d, cols)
                arrival(vrec.at[c, p], v_recv.at[c, p]).wait_recv()
            for i in range(per):
                lanes = slice(i * r_tile, (i + 1) * r_tile)
                total = acc[p * per + i, mine, :]
                for d in range(1, cols):
                    total += vrec[other(col, d, cols), p, :, lanes].astype(F32)
                start = p * cw + i * r_tile
                out_ref[:, start:start + r_tile] = total.astype(BF16)

    def up_compute():
        def lead_step(step, carry):
            b, p = lax.rem(step, ratio), cols + lax.div(step, ratio)
            arrived_g(1, b, p)

            @pl.when((step == 0) & (lay == last))
            def _():
                for k in range(2):
                    target = holder(late, k)
                    if target == last:
                        spread(k, incp.at[k], ginc, 0, k, late)
                    else:
                        pl.semaphore_signal(
                            go_sem, inc=1, device_id=(target, row, col), device_id_type=MESH
                        )

            lhs = gup[b, p].reshape(traces, cw)
            j = b * pieces + p

            @pl.when(lay == last)
            def _():
                for i in range(acc.shape[0]):
                    acc[i] += times(lhs, tv[j, pl.ds(i * r_tile, r_tile), :])

            @pl.when(lay < last)
            def _():
                for i in range(acc.shape[0]):
                    acc[i] += times_turned(lhs, j, i * r_tile)

            return carry

        lax.fori_loop(0, ratio * cols, lead_step, 0)
        for p in range(cols):
            for b in range(ratio):
                arrived_g(1, b, p)

        def piece_step(o, carry):
            k = 1 - lax.div(o, cols)
            y = other(col, cols - 1 - lax.rem(o, cols), cols)
            p = k * cols + y
            for i in range(per):
                tile = p * per + i
                start = pl.multiple_of(tile * r_tile, r_tile)
                total = acc[tile]
                for pp in range(cols):
                    for b in range(ratio):
                        total += times_turned(
                            gup[b, pp].reshape(traces, cw), b * pieces + pp, start
                        )
                acc[tile] = total

            @pl.when((o < pieces - 1) | (lay == 0))
            def _():
                for i in range(per):
                    ubuf[p, :, :, i * r_tile:(i + 1) * r_tile] = (
                        acc[p * per + i].astype(BF16).reshape(cols, part, r_tile)
                    )

            @pl.when((o < pieces - 1) & (lay > 0))
            def _():
                for h in range(cols):
                    u_copy(k, y, h).start()

            @pl.when(lay == 0)
            def _():
                for d in range(1, cols):
                    v_copy(other(col, d, cols), p).start()

            return carry

        lax.fori_loop(0, pieces, piece_step, 0)

    def o_copy(k, layer, c):
        p = k * cols + col
        return remote(natu.at[k, c], obuf.at[p], o_send.at[k, c], o_recv.at[p], (layer, row, c))

    def up_sum(l, k):
        for h in range(cols):
            for d in range(cols):
                if k or d:
                    c = other(col, d, cols)
                    arrival(urec.at[k, c, h], u_recv.at[k, c, h]).wait_recv()
            if k == 0:
                for i in range(per):
                    lanes = slice(i * r_tile, (i + 1) * r_tile)
                    total = acc[col * per + i, h * part:(h + 1) * part]
                    for d in range(1, cols):
                        total += urec[0, other(col, d, cols), h, :, lanes].astype(F32)
                    natu[0, h, :, lanes] = total.astype(BF16)
            else:
                natu[1, h] = jnp.sum(urec[1, :, h].astype(F32), axis=0).astype(BF16)

            spread_part(3 + k, natu.at[k], gup, 1, k, l - 1, h)

        for c in range(cols):
            mine = (k == 0) & (col == c)

            @pl.when(mine)
            def _():
                obuf[k * cols + col] = natu[k, c]

            @pl.when(jnp.logical_not(mine))
            def _():
                o_copy(k, l, c).start()

    def stage(t, carry):
        down = t < layers
        l = jnp.where(down, t, 2 * layers - 1 - t)

        @pl.when(down & (lay == l))
        def _():
            down_compute()

        m = jnp.where(l < last, l + 1, last - 1)
        for k in range(2):
            @pl.when(down & (lay == holder(m, k)))
            def _():
                @pl.when(l < last)
                def _():
                    got_s(k)

                down_sum(l, m, k)

        for k in range(2):
            @pl.when((t == layers) & (lay == holder(late, k)) & (lay != last))
            def _():
                pl.semaphore_wait(go_sem, 1)
                spread(k, incp.at[k], ginc, 0, k, late)

        @pl.when(t == jnp.where(lay == late, layers + 1, lax.min(lay + 2, layers)))
        def _():
            reflect()

        @pl.when(jnp.logical_not(down) & (lay == l))
        def _():
            up_compute()

        for k in range(2):
            @pl.when(jnp.logical_not(down) & (l > 0) & (lay == holder(l, k)))
            def _():
                up_sum(l, k)

        return carry

    lax.fori_loop(0, 2 * layers, stage, 0)

    @pl.when(lay == 0)
    def _():
        top_sum()

    @pl.when(lay > 0)
    def _():
        for k in range(2):
            for d in range(cols):
                if k or d:
                    p = k * cols + other(col, d, cols)
                    arrival(obuf.at[p], o_recv.at[p]).wait_recv()
        for p in range(pieces):
            out_ref[:, p * cw:(p + 1) * cw] = obuf[p]

    @pl.when(lay == 0)
    def _():
        for p in range(pieces):
            for d in range(1, cols):
                first_copy(other(col, d, cols), p).wait_send()
                v_copy(other(col, d, cols), p).wait_send()

    for k in range(2):
        for d in range(cols):
            if k or d:
                y = other(col, d, cols)
                s_copy(k, y).wait_send()

                @pl.when(lay > 0)
                def _():
                    for h in range(cols):
                        u_copy(k, y, h).wait_send()
    for step in range(chunks):
        for h in range(cols):
            d_copy(step, h)[1].wait_send()

    def sums_sent(l, m, k):
        q = jnp.where(l == last, 2, k)
        same = plane(l) == plane(lay)
        for d in range(cols):
            c = other(col, d, cols)
            for b in range(ratio):
                for h in range(cols):
                    goal, copy = f_copy(q, c, b, h)
                    sent = goal != row
                    if d == 0:
                        sent = sent & jnp.logical_not(same)

                    @pl.when(sent)
                    def _():
                        copy.wait_send()

        if k == 0:
            @pl.when(l < last)
            def _():
                for d in range(1, cols):
                    for h in range(cols):
                        n_copy(k, m, other(col, d, cols), h).wait_send()

    def stage_sent(l, carry):
        m = jnp.where(l < last, l + 1, last - 1)
        for k in range(2):
            @pl.when(lay == holder(m, k))
            def _():
                sums_sent(l, m, k)

                @pl.when(l == last)
                def _():
                    spread_sent(2, incp.at[2], gup, 1, k, last)

            @pl.when(lay == holder(l, k))
            def _():
                spread_sent(k, incp.at[k], ginc, 0, k, l)

                @pl.when(l > 0)
                def _():
                    spread_sent(3 + k, natu.at[k], gup, 1, k, l - 1)
                    for c in range(cols):
                        @pl.when(jnp.logical_not((k == 0) & (col == c)))
                        def _():
                            o_copy(k, l, c).wait_send()

        return carry

    lax.fori_loop(0, layers, stage_sent, 0)


def per_device(layers, rows, cols, sources, transmission, reflection):
    ratio = rows // cols
    own, width = sources.shape[1], sources.shape[2]
    pieces = 2 * cols
    if layers % 2 or layers < 4 or rows % cols or width % (pieces * 128):
        return plain_per_device(layers, rows, cols, sources, transmission, reflection)
    part = -(-own // 16) * 16
    cw = width // pieces
    chunks = ratio * pieces
    r_tile = 256 if cw % 256 == 0 else 128
    traces = cols * part
    src = jnp.pad(sources[0], ((0, part - own), (0, 0)))
    dma, vmem = pltpu.SemaphoreType.DMA, pltpu.VMEM
    result = pl.pallas_call(
        functools.partial(kernel, layers, rows, cols, r_tile),
        out_shape=jax.ShapeDtypeStruct((part, width), BF16),
        in_specs=[
            pl.BlockSpec(memory_space=pltpu.VMEM),
            pl.BlockSpec(memory_space=pl.ANY),
            pl.BlockSpec(memory_space=pl.ANY),
        ],
        out_specs=pl.BlockSpec(memory_space=pltpu.VMEM),
        scratch_shapes=[
            vmem((chunks, width, cw), BF16),
            vmem((2, width, cw), BF16),
            vmem((pieces, part, cw), BF16),
            vmem((2, cols, part, cw), BF16),
            vmem((pieces, cols, part, cw), BF16),
            vmem((chunks, cols, part, cw), BF16),
            vmem((3, cols, ratio, cols, part, cw), BF16),
            vmem((3, rows, cols, part, cw), BF16),
            vmem((3, cols, part, cw), BF16),
            vmem((ratio, pieces, cols, part, cw), BF16),
            vmem((ratio, pieces, cols, part, cw), BF16),
            vmem((width // r_tile, traces, r_tile), F32),
            vmem((pieces, cols, part, cw), BF16),
            vmem((2, cols, cols, part, cw), BF16),
            vmem((2, cols, part, cw), BF16),
            vmem((pieces, part, cw), BF16),
            vmem((cols, pieces, part, cw), BF16),
            dma((chunks,)), dma((2,)),
            dma((2, cols)), dma((2, cols)),
            dma((cols, pieces)), dma((cols, pieces)),
            dma((chunks, cols)), dma((3, cols, ratio, cols)),
            dma((3, cols, ratio, cols)), dma((3, rows, cols)),
            dma((2, cols, cols)), dma((pieces, cols)),
            dma((5, rows, cols)), dma((2, ratio, pieces, cols)),
            dma((pieces, cols)), dma((2, cols, cols)), dma((2, cols)), dma((pieces,)),
            dma((cols, pieces)), dma((cols, pieces)), pltpu.SemaphoreType.REGULAR,
        ],
        compiler_params=pltpu.CompilerParams(
            collective_id=0, has_side_effects=True, vmem_limit_bytes=66_000_000
        ),
    )(src, transmission[0], reflection[0])
    return result[None, :own]


def plain_kernel(
    layers, rows, cols, pieces, r_tile,
    src_ref, trans_ref, refl_ref, out_ref,
    tv, rbuf, sall, nin, incn, pbuf, ybuf, zbuf, natd, natu, ginc, gup, acc, ubuf, urec,
    t_sem, r_sem, s_send, s_recv, n_send, n_recv, y_send, y_recv, z_send, z_recv,
    g_send, g_recv, u_send, u_recv, go_sem,
):
    ratio = rows // cols
    chunks = ratio * pieces
    lay, row, col = (lax.axis_index(name) for name in ("layer", "row", "col"))
    part, cw = natd.shape[1], natd.shape[2]
    traces = cols * part
    tiles = acc.shape[0]
    last = layers - 1
    home_col, home_b = lax.div(row, ratio), lax.rem(row, ratio)

    def other(index, by, size):
        return lax.rem(index + by, size)

    def remote(src, dst, send, recv, target):
        return pltpu.make_async_remote_copy(
            src_ref=src, dst_ref=dst, send_sem=send, recv_sem=recv,
            device_id=target, device_id_type=MESH,
        )

    def column_block(step):
        return lax.rem(step, ratio) * pieces + lax.div(step, ratio)

    def t_copy(j):
        start = pl.multiple_of(j * cw, 128)
        return pltpu.make_async_copy(trans_ref.at[:, pl.ds(start, cw)], tv.at[j], t_sem.at[j])

    def r_copy(step):
        start = pl.multiple_of(column_block(step) * cw, 128)
        slot = lax.rem(step, 2)
        return pltpu.make_async_copy(
            refl_ref.at[:, pl.ds(start, cw)], rbuf.at[slot], r_sem.at[slot]
        )

    def copy_src(c):
        return remote(sall.at[col], sall.at[col], s_send.at[c], s_recv.at[col], (lay, row, c))

    def got_src(c):
        return remote(sall.at[c], sall.at[c], s_send.at[c], s_recv.at[c], (lay, row, c))

    def copy_next(c, p):
        return remote(natd.at[p], nin.at[col, p], n_send.at[c, p], n_recv.at[col, p],
                      (lax.min(lay + 1, last), row, c))

    def got_next(c, p):
        return remote(natd.at[p], nin.at[c, p], n_send.at[c, p], n_recv.at[c, p],
                      (lax.max(lay - 1, 0), row, c))

    def copy_y(c, j):
        return remote(pbuf.at[j, c], ybuf.at[col, j], y_send.at[c, j], y_recv.at[col, j],
                      (lay, row, c))

    def got_y(c, j):
        return remote(pbuf.at[j, c], ybuf.at[c, j], y_send.at[c, j], y_recv.at[c, j],
                      (lay, row, c))

    def copy_z(c, j, own):
        block = pbuf.at[j, col] if own else ybuf.at[c, j]
        goal = ratio * c + lax.div(j, pieces)
        return goal, block, remote(
            block, zbuf.at[row, lax.rem(j, pieces)], z_send.at[c, j],
            z_recv.at[row, lax.rem(j, pieces)], (lay, goal, col),
        )

    def got_z(r, p):
        return remote(natd.at[p], zbuf.at[r, p], z_send.at[0, 0], z_recv.at[r, p],
                      (lay, r, col))

    def copy_g(which, p, r):
        block = incn.at[p, col] if which == 0 else (natd, natu)[which - 1].at[p]
        buf, slot = (ginc, 0) if which == 0 else (gup, 1)
        target = lax.max(lay - 1, 0) if which == 2 else lay
        return block, buf, remote(
            block, buf.at[home_b, p, col], g_send.at[which, p, r],
            g_recv.at[slot, p, home_b, col], (target, r, home_col),
        )

    def got_g(slot, p, b, c):
        buf = gup if slot else ginc
        return remote(natd.at[p], buf.at[b, p, c], g_send.at[0, 0, 0],
                      g_recv.at[slot, p, b, c], (lay, ratio * col + b, c))

    def send_g(which, p):
        for d in range(1, rows):
            copy_g(which, p, other(row, d, rows))[2].start()
        block, buf, copy = copy_g(which, p, row)
        if which == 2:
            copy.start()
            return

        @pl.when(home_col == col)
        def _():
            buf[home_b, p, col] = block[...]

        @pl.when(home_col != col)
        def _():
            copy.start()

    def sent_g(which, p):
        for d in range(1, rows):
            copy_g(which, p, other(row, d, rows))[2].wait_send()
        copy = copy_g(which, p, row)[2]
        if which == 2:
            copy.wait_send()
            return

        @pl.when(home_col != col)
        def _():
            copy.wait_send()

    def arrived_g(slot, p, b):
        for c in range(cols):
            mine = (ratio * col + b == row) & (col == c)
            if slot:
                mine = mine & (lay == last)

            @pl.when(jnp.logical_not(mine))
            def _():
                got_g(slot, p, b, c).wait_recv()

    def copy_u(c, p):
        return remote(ubuf.at[c, p], urec.at[col, p], u_send.at[c, p], u_recv.at[col, p],
                      (lay, row, c))

    def got_u(c, p):
        return remote(ubuf.at[c, p], urec.at[c, p], u_send.at[c, p], u_recv.at[c, p],
                      (lay, row, c))

    for step in range(chunks):
        t_copy((step % ratio) * pieces + step // ratio).start()

    barrier = pltpu.get_barrier_semaphore()

    def greet(target):
        pl.semaphore_signal(barrier, inc=1, device_id=target, device_id_type=MESH)

    for dr in range(rows):
        for dc in range(cols):
            if dr or dc:
                greet((lay, other(row, dr, rows), other(col, dc, cols)))

    @pl.when(lay > 0)
    def _():
        for r in range(rows):
            for c in range(cols):
                greet((lay - 1, r, c))

    @pl.when(lay < last)
    def _():
        for r in range(rows):
            for c in range(cols):
                greet((lay + 1, r, c))

    near = (lay > 0).astype(jnp.int32) + (lay < last).astype(jnp.int32)
    pl.semaphore_wait(barrier, rows * cols - 1 + rows * cols * near)

    for p in range(pieces):
        sall[col, p] = src_ref[:, p * cw:(p + 1) * cw]
    for d in range(1, cols):
        copy_src(other(col, d, cols)).start()
    for step in range(2):
        r_copy(step).start()
    acc[...] = jnp.zeros_like(acc)
    for d in range(1, cols):
        got_src(other(col, d, cols)).wait_recv()

    @pl.when(lay == 0)
    def _():
        for p in range(pieces):
            incn[p] = sall[:, p]

    @pl.when(lay > 0)
    def _():
        for p in range(pieces):
            for c in range(cols):
                got_next(c, p).wait_recv()
            incn[p] = (nin[:, p].astype(F32) + sall[:, p].astype(F32)).astype(BF16)

    def to_row(c, j, own):
        goal, block, copy = copy_z(c, j, own)

        @pl.when(goal == row)
        def _():
            zbuf[row, lax.rem(j, pieces)] = block[...]

        @pl.when(goal != row)
        def _():
            copy.start()

    def forward(j):
        for d in range(1, cols):
            c = other(col, d, cols)
            got_y(c, j).wait_recv()
            to_row(c, j, False)

    def down_step(step, carry):
        j = column_block(step)
        t_copy(j).wait()
        total = jnp.zeros((traces, cw), F32)
        for p in range(pieces):
            total += jnp.dot(
                incn[p].reshape(traces, cw), tv[j, pl.ds(p * cw, cw), :],
                preferred_element_type=F32,
            )
        pbuf[j] = total.astype(BF16).reshape(cols, part, cw)
        for d in range(1, cols):
            copy_y(other(col, d, cols), j).start()
        to_row(col, j, True)

        @pl.when(step > 0)
        def _():
            forward(column_block(step - 1))

        return carry

    lax.fori_loop(0, chunks, down_step, 0)
    forward(column_block(chunks - 1))

    @pl.when(lay == last)
    def _():
        for p in range(pieces):
            send_g(0, p)

    for p in range(pieces):
        for d in range(1, rows):
            got_z(other(row, d, rows), p).wait_recv()
        natd[p] = jnp.sum(zbuf[:, p].astype(F32), axis=0).astype(BF16)

        @pl.when(lay < last)
        def _():
            for c in range(cols):
                copy_next(c, p).start()

        @pl.when(lay == last)
        def _():
            send_g(1, p)

    def signal_go():
        pl.semaphore_signal(
            go_sem, inc=1, device_id=(lay - 1, row, col), device_id_type=MESH
        )

    @pl.when((lay > 0) & (lay < last))
    def _():
        signal_go()

    @pl.when(lay < last)
    def _():
        early = pieces // 2
        for p in range(early):
            send_g(0, p)
        pl.semaphore_wait(go_sem, 1)
        for p in range(early, pieces):
            send_g(0, p)

    contract = (((1,), (1,)), ((), ()))

    def times(lhs, rhs):
        return lax.dot_general(lhs, rhs, contract, preferred_element_type=F32)

    def add_product(lhs, weights):
        for i in range(tiles):
            acc[i] += times(lhs, weights[pl.ds(i * r_tile, r_tile), :])

    def reflect_step(step, carry):
        b, p = lax.rem(step, ratio), lax.div(step, ratio)
        arrived_g(0, p, b)
        r_copy(step).wait()
        add_product(ginc[b, p].reshape(traces, cw), rbuf.at[lax.rem(step, 2)])

        @pl.when(step + 2 < chunks)
        def _():
            r_copy(step + 2).start()

        return carry

    lax.fori_loop(0, chunks, reflect_step, 0)

    def up_step(step, carry):
        b, p = lax.rem(step, ratio), lax.div(step, ratio)
        arrived_g(1, p, b)
        add_product(gup[b, p].reshape(traces, cw), tv.at[b * pieces + p])
        return carry

    lax.fori_loop(0, chunks - ratio, up_step, 0)
    end = pieces - 1
    for b in range(ratio):
        arrived_g(1, end, b)

    @pl.when((lay > 0) & (lay == last))
    def _():
        signal_go()

    per = cw // r_tile

    def piece_of(p, c):
        found = []
        for i in range(per):
            found.append(acc[p * per + i, pl.ds(pl.multiple_of(c * part, 8), part), :])
        return jnp.concatenate(found, axis=1)

    for p in range(pieces):
        for i in range(p * per, (p + 1) * per):
            total = acc[i]
            for b in range(ratio):
                total += times(
                    gup[b, end].reshape(traces, cw),
                    tv[b * pieces + end, pl.ds(i * r_tile, r_tile), :],
                )
            acc[i] = total
        for d in range(1, cols):
            c = other(col, d, cols)
            ubuf[c, p] = piece_of(p, c).astype(BF16)
            copy_u(c, p).start()

    for p in range(pieces):
        total = piece_of(p, col)
        for d in range(1, cols):
            c = other(col, d, cols)
            got_u(c, p).wait_recv()
            total += urec[c, p].astype(F32)
        result = total.astype(BF16)
        natu[p] = result
        out_ref[:, p * cw:(p + 1) * cw] = result

        @pl.when(lay > 0)
        def _():
            send_g(2, p)

    for d in range(1, cols):
        c = other(col, d, cols)
        copy_src(c).wait_send()
        for p in range(pieces):
            copy_u(c, p).wait_send()
        for j in range(chunks):
            copy_y(c, j).wait_send()
    for d in range(cols):
        c = other(col, d, cols)
        for j in range(chunks):
            goal, _, copy = copy_z(c, j, d == 0)

            @pl.when(goal != row)
            def _():
                copy.wait_send()

    for p in range(pieces):
        sent_g(0, p)

        @pl.when(lay < last)
        def _():
            for c in range(cols):
                copy_next(c, p).wait_send()

        @pl.when(lay == last)
        def _():
            sent_g(1, p)

        @pl.when(lay > 0)
        def _():
            sent_g(2, p)


def split_of(width):
    for pieces in (4, 3, 2):
        if width % (pieces * 128) == 0:
            return pieces
    return 1


def plain_per_device(layers, rows, cols, sources, transmission, reflection):
    ratio = rows // cols
    own, width = sources.shape[1], sources.shape[2]
    part = -(-own // 16) * 16
    pieces = split_of(width)
    cw = width // pieces
    chunks = ratio * pieces
    r_tile = 256 if cw % 256 == 0 else 128
    traces = cols * part
    src = jnp.pad(sources[0], ((0, part - own), (0, 0)))
    dma, vmem = pltpu.SemaphoreType.DMA, pltpu.VMEM
    result = pl.pallas_call(
        functools.partial(plain_kernel, layers, rows, cols, pieces, r_tile),
        out_shape=jax.ShapeDtypeStruct((part, width), BF16),
        in_specs=[
            pl.BlockSpec(memory_space=pltpu.VMEM),
            pl.BlockSpec(memory_space=pl.ANY),
            pl.BlockSpec(memory_space=pl.ANY),
        ],
        out_specs=pl.BlockSpec(memory_space=pltpu.VMEM),
        scratch_shapes=[
            vmem((chunks, width, cw), BF16),
            vmem((2, width, cw), BF16),
            vmem((cols, pieces, part, cw), BF16),
            vmem((cols, pieces, part, cw), BF16),
            vmem((pieces, cols, part, cw), BF16),
            vmem((chunks, cols, part, cw), BF16),
            vmem((cols, chunks, part, cw), BF16),
            vmem((rows, pieces, part, cw), BF16),
            vmem((pieces, part, cw), BF16),
            vmem((pieces, part, cw), BF16),
            vmem((ratio, pieces, cols, part, cw), BF16),
            vmem((ratio, pieces, cols, part, cw), BF16),
            vmem((width // r_tile, traces, r_tile), F32),
            vmem((cols, pieces, part, cw), BF16),
            vmem((cols, pieces, part, cw), BF16),
            dma((chunks,)), dma((2,)),
            dma((cols,)), dma((cols,)),
            dma((cols, pieces)), dma((cols, pieces)),
            dma((cols, chunks)), dma((cols, chunks)),
            dma((cols, chunks)), dma((rows, pieces)),
            dma((3, pieces, rows)), dma((2, pieces, ratio, cols)),
            dma((cols, pieces)), dma((cols, pieces)),
            pltpu.SemaphoreType.REGULAR,
        ],
        compiler_params=pltpu.CompilerParams(
            collective_id=0, has_side_effects=True, vmem_limit_bytes=66_000_000
        ),
    )(src, transmission[0], reflection[0])
    return result[None, :own]


def solution(mesh):
    sizes = [mesh.shape[name] for name in ("layer", "row", "col")]
    return jax.shard_map(
        functools.partial(per_device, *sizes),
        mesh=mesh,
        in_specs=(P("layer", "col", "row"), P("layer", "row", "col"), P("layer", "row", "col")),
        out_specs=P("layer", "col", "row"),
        check_vma=False,
    )
```

```python
import functools

import jax
import jax.numpy as jnp
from jax import lax
from jax.experimental import pallas as pl
from jax.experimental.pallas import tpu as pltpu
from jax.sharding import PartitionSpec as P

MESH = pl.DeviceIdType.MESH
BF16 = jnp.bfloat16
F32 = jnp.float32


def kernel(
    layers, rows, cols, r_tile,
    src_ref, trans_ref, refl_ref, out_ref,
    tv, rbuf, ssend, sp, incn, pbuf, rel, zbuf, incp, ginc, gup, acc, ubuf, urec, natu, obuf, vrec, acct,
    t_sem, r_sem, s_send, s_recv, i_send, i_recv, d_send, rel_recv, f_send, z_recv,
    n_send, n_recv, g_send, g_recv, u_send, u_recv, o_send, o_recv, v_send, v_recv, go_sem,
):
    ratio = rows // cols
    half = layers // 2
    pieces = 2 * cols
    chunks = ratio * pieces
    lay, row, col = (lax.axis_index(name) for name in ("layer", "row", "col"))
    part, cw = pbuf.shape[2], pbuf.shape[3]
    traces = cols * part
    per = cw // r_tile
    last = layers - 1
    late = last - 2
    home_col, home_b = lax.div(row, ratio), lax.rem(row, ratio)

    def other(index, by, size):
        return lax.rem(index + by, size)

    def peer(layer):
        return lax.rem(layer + half, layers)

    def holder(layer, k):
        if isinstance(layer, int):
            return (layer + k * half) % layers
        return lax.rem(layer + k * half, layers)

    def plane(layer):
        return lax.div(layer, half)

    def remote(src, dst, send, recv, target):
        return pltpu.make_async_remote_copy(
            src_ref=src, dst_ref=dst, send_sem=send, recv_sem=recv,
            device_id=target, device_id_type=MESH,
        )

    me = (lay, row, col)
    up_peer = lax.rem(lay + 1, layers)

    def arrival(dst, recv):
        return remote(dst, dst, recv, recv, (up_peer, row, col))

    base = jnp.where(lay < last, lay + 1, last - 1)
    near_k = jnp.where(plane(base) == plane(lay), 0, 1)

    def order(step):
        o, b = lax.div(step, ratio), lax.rem(step, ratio)
        near = lax.div(o, cols)
        d = cols - 1 - lax.rem(o, cols)
        k = jnp.where(near == 1, near_k, 1 - near_k)
        y = other(col, d, cols)
        return near, d, k, y, b, k * cols + y

    def t_copy(j):
        start = pl.multiple_of(j * cw, 128)
        return pltpu.make_async_copy(trans_ref.at[:, pl.ds(start, cw)], tv.at[j], t_sem.at[j])

    def r_index(step):
        p, b = lax.div(step, ratio), lax.rem(step, ratio)
        return b, p

    def r_copy(step):
        b, p = r_index(step)
        start = pl.multiple_of((b * pieces + p) * cw, 128)
        slot = lax.rem(step, 2)
        return pltpu.make_async_copy(
            refl_ref.at[:, pl.ds(start, cw)], rbuf.at[slot], r_sem.at[slot]
        )

    for step in range(chunks):
        b, p = order(step)[-2:]
        t_copy(b * pieces + p).start()

    barrier = pltpu.get_barrier_semaphore()
    for dl in range(layers):
        for dr in range(rows):
            for dc in range(cols):
                if dl or dr or dc:
                    pl.semaphore_signal(
                        barrier, inc=1, device_id_type=MESH,
                        device_id=(other(lay, dl, layers), other(row, dr, rows), other(col, dc, cols)),
                    )
    pl.semaphore_wait(barrier, layers * rows * cols - 1)

    for k in range(2):
        for y in range(cols):
            p = k * cols + y
            ssend[p] = src_ref[:, p * cw:(p + 1) * cw]

    def first_copy(c, p):
        return remote(ssend.at[p], incn.at[p, col], i_send.at[c, p], i_recv.at[col, p], (lay, row, c))

    @pl.when(lay == 0)
    def _():
        for p in range(pieces):
            for d in range(1, cols):
                first_copy(other(col, d, cols), p).start()
            incn[p, col] = ssend[p]

    def s_copy(k, y):
        return remote(ssend.at[k * cols + y], sp.at[k, col], s_send.at[k, y], s_recv.at[k, col],
                      (holder(lay, k), row, y))

    for k in (1, 0):
        for d in range(cols):
            if k or d:
                s_copy(k, other(col, d, cols)).start()
    sp[0, col] = ssend[col]
    acc[...] = jnp.zeros_like(acc)
    acct[...] = jnp.zeros_like(acct)

    def got_s(k):
        for d in range(cols):
            if k or d:
                c = other(col, d, cols)
                arrival(sp.at[k, c], s_recv.at[k, c]).wait_recv()

    def g_copy(slot, block, buf, which, k, layer, r, h):
        p = k * cols + col
        if which == 0:
            return remote(block, buf.at[home_b, p], g_send.at[slot, r, h],
                          g_recv.at[which, home_b, p, h], (layer, r, home_col))
        return remote(block.at[h], buf.at[home_b, p, h], g_send.at[slot, r, h],
                      g_recv.at[which, home_b, p, h], (layer, r, home_col))

    def spread_part(slot, block, buf, which, k, layer, h):
        for d in range(1, rows):
            g_copy(slot, block, buf, which, k, layer, other(row, d, rows), h).start()
        mine = (layer == lay) & (home_col == col)

        @pl.when(mine)
        def _():
            if which == 0:
                buf[home_b, k * cols + col] = block[...]
            else:
                buf[home_b, k * cols + col, h] = block[h]

        @pl.when(jnp.logical_not(mine))
        def _():
            g_copy(slot, block, buf, which, k, layer, row, h).start()

    def spread(slot, block, buf, which, k, layer):
        for h in range(cols if which else 1):
            spread_part(slot, block, buf, which, k, layer, h)

    def spread_sent(slot, block, buf, which, k, layer):
        for h in range(cols if which else 1):
            for d in range(1, rows):
                g_copy(slot, block, buf, which, k, layer, other(row, d, rows), h).wait_send()

            @pl.when(jnp.logical_not((layer == lay) & (home_col == col)))
            def _():
                g_copy(slot, block, buf, which, k, layer, row, h).wait_send()

    def arrived_g(which, b, p):
        buf = gup if which else ginc
        if which:
            for h in range(cols):
                arrival(buf.at[b, p, h], g_recv.at[which, b, p, h]).wait_recv()
            return
        mine = (ratio * col + b == row) & (p == col)

        @pl.when(jnp.logical_not(mine))
        def _():
            arrival(buf.at[b, p], g_recv.at[which, b, p, 0]).wait_recv()

    for k in range(2):
        @pl.when(lay == k * half)
        def _():
            got_s(k)
            incp[k] = sp[k]
            if k:
                spread(k, incp.at[k], ginc, 0, k, 0)

    def d_copy(step, h):
        near, d, k, y, b, p = order(step)
        j = b * pieces + p
        q = jnp.where(lay == last, 2, k)
        target = holder(base, k)
        direct = (near == 1) & (d == 0)
        return direct, remote(
            pbuf.at[j, h], zbuf.at[q, row, h], d_send.at[j, h], z_recv.at[q, row, h],
            (target, ratio * col + b, col),
        ), remote(
            pbuf.at[j, h], rel.at[q, col, b, h], d_send.at[j, h], rel_recv.at[q, col, b, h],
            (target, row, y),
        )

    def down_compute():
        @pl.when(lay == 0)
        def _():
            for p in range(pieces):
                for d in range(1, cols):
                    c = other(col, d, cols)
                    arrival(incn.at[p, c], i_recv.at[c, p]).wait_recv()
            spread(0, incp.at[0], ginc, 0, 0, 0)

        @pl.when(lay > 0)
        def _():
            for k in range(2):
                for d in range(cols):
                    if k or d:
                        p = k * cols + other(col, d, cols)
                        for h in range(cols):
                            arrival(incn.at[p, h], n_recv.at[p, h]).wait_recv()

            @pl.when(lay != late)
            def _():
                spread(0, incp.at[0], ginc, 0, 0, lay)

        def down_step(step, carry):
            b, p = order(step)[-2:]
            j = b * pieces + p
            t_copy(j).wait()
            total = jnp.zeros((traces, cw), F32)
            for i in range(pieces):
                total += jnp.dot(
                    incn[i].reshape(traces, cw), tv[j, pl.ds(i * cw, cw), :],
                    preferred_element_type=F32,
                )
            pbuf[j] = total.astype(BF16).reshape(cols, part, cw)
            for h in range(cols):
                direct, straight, relayed = d_copy(step, h)

                @pl.when(direct)
                def _():
                    straight.start()

                @pl.when(jnp.logical_not(direct))
                def _():
                    relayed.start()

            return carry

        lax.fori_loop(0, chunks, down_step, 0)
        for step in range(2):
            r_copy(step).start()

        tiles = acc.shape[0]

        def turn_step(step, carry):
            at, i = lax.div(step, tiles), lax.rem(step, tiles)
            j = lax.rem(at, ratio) * pieces + lax.div(at, ratio)
            rows_at = pl.ds(pl.multiple_of(i * r_tile, r_tile), r_tile)
            turned = [tv[j, rows_at, n * r_tile:(n + 1) * r_tile].T for n in range(per)]
            for n in range(per):
                tv[j, rows_at, n * r_tile:(n + 1) * r_tile] = turned[n]
            return carry

        turns = jnp.where(lay == last, cols, pieces) * (ratio * tiles)
        lax.fori_loop(0, turns, turn_step, 0)

    def f_copy(q, c, b, h):
        goal = ratio * c + b
        return goal, remote(rel.at[q, c, b, h], zbuf.at[q, row, h], f_send.at[q, c, b, h],
                            z_recv.at[q, row, h], (lay, goal, col))

    def n_copy(k, layer, c, h):
        p = k * cols + col
        return remote(incp.at[k, h], incn.at[p, h], n_send.at[k, c, h], n_recv.at[p, h],
                      (layer, row, c))

    def forward(q, c):
        for b in range(ratio):
            for h in range(cols):
                arrival(rel.at[q, c, b, h], rel_recv.at[q, c, b, h]).wait_recv()
                goal, copy = f_copy(q, c, b, h)

                @pl.when(goal == row)
                def _():
                    zbuf[q, row, h] = rel[q, c, b, h]

                @pl.when(goal != row)
                def _():
                    copy.start()

    def down_sum(l, m, k):
        q = jnp.where(l == last, 2, k)
        same = plane(l) == plane(lay)
        for d in range(1, cols):
            forward(q, other(col, d, cols))

        @pl.when(jnp.logical_not(same))
        def _():
            forward(q, col)

        for h in range(cols):
            for d in range(rows):
                r = other(row, d, rows)
                if d:
                    arrival(zbuf.at[q, r, h], z_recv.at[q, r, h]).wait_recv()
                else:
                    @pl.when(same & (home_col == col))
                    def _():
                        arrival(zbuf.at[q, r, h], z_recv.at[q, r, h]).wait_recv()

            down = jnp.sum(zbuf[q, :, h].astype(F32), axis=0).astype(BF16)

            @pl.when(l < last)
            def _():
                incp[k, h] = (down.astype(F32) + sp[k, h].astype(F32)).astype(BF16)
                for d in range(1, cols):
                    n_copy(k, m, other(col, d, cols), h).start()
                if k:
                    n_copy(k, m, col, h).start()
                else:
                    incn[col, h] = incp[k, h]

            @pl.when(l == last)
            def _():
                incp[2, h] = down
                spread_part(2, incp.at[2], gup, 1, k, last, h)

        if k == 1:
            @pl.when(l < last)
            def _():
                for c in range(cols):
                    for h in range(cols):
                        n_copy(k, m, c, h).wait_send()

                @pl.when(m != late)
                def _():
                    spread(k, incp.at[k], ginc, 0, k, m)

    contract = (((1,), (1,)), ((), ()))

    def times(lhs, rhs):
        return lax.dot_general(lhs, rhs, contract, preferred_element_type=F32)

    def add_products(lhs, weights):
        for i in range(acc.shape[0]):
            tile = weights[pl.ds(i * r_tile, r_tile), :]
            if i % 3 == 1:
                acct[i // 3] += times(tile, lhs)
            else:
                acc[i] += times(lhs, tile)

    def turn_products():
        for q in range(acct.shape[0]):
            acc[3 * q + 1] += acct[q].T

    def reflect():
        def reflect_step(step, carry):
            b, p = r_index(step)
            arrived_g(0, b, p)
            r_copy(step).wait()
            lhs = ginc[b, p].reshape(traces, cw)
            slot = lax.rem(step, 2)
            add_products(lhs, rbuf.at[slot])

            @pl.when(step + 2 < chunks)
            def _():
                r_copy(step + 2).start()

            return carry

        lax.fori_loop(0, chunks, reflect_step, 0)

        @pl.when(lay < last)
        def _():
            turn_products()

    def u_copy(k, y, h):
        p = k * cols + y
        return remote(ubuf.at[p, h], urec.at[k, col, h], u_send.at[p, h], u_recv.at[k, col, h],
                      (holder(lay, k), row, y))

    def times_turned(lhs, j, start):
        total = None
        for n in range(per):
            term = jnp.dot(
                lhs[:, n * r_tile:(n + 1) * r_tile],
                tv[j, pl.ds(start, r_tile), n * r_tile:(n + 1) * r_tile],
                preferred_element_type=F32,
            )
            total = term if total is None else total + term
        return total

    def v_copy(c, p):
        return remote(ubuf.at[p, c], vrec.at[col, p], v_send.at[c, p], v_recv.at[col, p],
                      (lay, row, c))

    def top_sum():
        mine = pl.ds(pl.multiple_of(col * part, 16), part)
        for p in list(range(cols, pieces)) + list(range(cols)):
            for d in range(1, cols):
                c = other(col, d, cols)
                arrival(vrec.at[c, p], v_recv.at[c, p]).wait_recv()
            for i in range(per):
                lanes = slice(i * r_tile, (i + 1) * r_tile)
                total = acc[p * per + i, mine, :]
                for d in range(1, cols):
                    total += vrec[other(col, d, cols), p, :, lanes].astype(F32)
                start = p * cw + i * r_tile
                out_ref[:, start:start + r_tile] = total.astype(BF16)

    def up_compute():
        def lead_step(step, carry):
            b, p = lax.rem(step, ratio), cols + lax.div(step, ratio)
            arrived_g(1, b, p)

            @pl.when((step == 0) & (lay == last))
            def _():
                for k in range(2):
                    target = holder(late, k)
                    if target == last:
                        spread(k, incp.at[k], ginc, 0, k, late)
                    else:
                        pl.semaphore_signal(
                            go_sem, inc=1, device_id=(target, row, col), device_id_type=MESH
                        )

            lhs = gup[b, p].reshape(traces, cw)
            j = b * pieces + p

            @pl.when(lay == last)
            def _():
                add_products(lhs, tv.at[j])

            @pl.when(lay < last)
            def _():
                for i in range(acc.shape[0]):
                    acc[i] += times_turned(lhs, j, i * r_tile)

            return carry

        lax.fori_loop(0, ratio * cols, lead_step, 0)

        @pl.when(lay == last)
        def _():
            turn_products()

        for p in range(cols):
            for b in range(ratio):
                arrived_g(1, b, p)

        def piece_step(o, carry):
            k = 1 - lax.div(o, cols)
            y = other(col, cols - 1 - lax.rem(o, cols), cols)
            p = k * cols + y
            for i in range(per):
                tile = p * per + i
                start = pl.multiple_of(tile * r_tile, r_tile)
                total = acc[tile]
                for pp in range(cols):
                    for b in range(ratio):
                        total += times_turned(
                            gup[b, pp].reshape(traces, cw), b * pieces + pp, start
                        )
                acc[tile] = total

            @pl.when((o < pieces - 1) | (lay == 0))
            def _():
                for i in range(per):
                    ubuf[p, :, :, i * r_tile:(i + 1) * r_tile] = (
                        acc[p * per + i].astype(BF16).reshape(cols, part, r_tile)
                    )

            @pl.when((o < pieces - 1) & (lay > 0))
            def _():
                for h in range(cols):
                    u_copy(k, y, h).start()

            @pl.when(lay == 0)
            def _():
                for d in range(1, cols):
                    v_copy(other(col, d, cols), p).start()

            return carry

        lax.fori_loop(0, pieces, piece_step, 0)

    def o_copy(k, layer, c):
        p = k * cols + col
        return remote(natu.at[k, c], obuf.at[p], o_send.at[k, c], o_recv.at[p], (layer, row, c))

    def up_sum(l, k):
        for h in range(cols):
            for d in range(cols):
                if k or d:
                    c = other(col, d, cols)
                    arrival(urec.at[k, c, h], u_recv.at[k, c, h]).wait_recv()
            if k == 0:
                for i in range(per):
                    lanes = slice(i * r_tile, (i + 1) * r_tile)
                    total = acc[col * per + i, h * part:(h + 1) * part]
                    for d in range(1, cols):
                        total += urec[0, other(col, d, cols), h, :, lanes].astype(F32)
                    natu[0, h, :, lanes] = total.astype(BF16)
            else:
                natu[1, h] = jnp.sum(urec[1, :, h].astype(F32), axis=0).astype(BF16)

            spread_part(3 + k, natu.at[k], gup, 1, k, l - 1, h)

        for c in range(cols):
            mine = (k == 0) & (col == c)

            @pl.when(mine)
            def _():
                obuf[k * cols + col] = natu[k, c]

            @pl.when(jnp.logical_not(mine))
            def _():
                o_copy(k, l, c).start()

    def stage(t, carry):
        down = t < layers
        l = jnp.where(down, t, 2 * layers - 1 - t)

        @pl.when(down & (lay == l))
        def _():
            down_compute()

        m = jnp.where(l < last, l + 1, last - 1)
        for k in range(2):
            @pl.when(down & (lay == holder(m, k)))
            def _():
                @pl.when(l < last)
                def _():
                    got_s(k)

                down_sum(l, m, k)

        for k in range(2):
            @pl.when((t == layers) & (lay == holder(late, k)) & (lay != last))
            def _():
                pl.semaphore_wait(go_sem, 1)
                spread(k, incp.at[k], ginc, 0, k, late)

        @pl.when(t == jnp.where(lay == late, layers + 1, lax.min(lay + 2, layers)))
        def _():
            reflect()

        @pl.when(jnp.logical_not(down) & (lay == l))
        def _():
            up_compute()

        for k in range(2):
            @pl.when(jnp.logical_not(down) & (l > 0) & (lay == holder(l, k)))
            def _():
                up_sum(l, k)

        return carry

    lax.fori_loop(0, 2 * layers, stage, 0)

    @pl.when(lay == 0)
    def _():
        top_sum()

    @pl.when(lay > 0)
    def _():
        for k in range(2):
            for d in range(cols):
                if k or d:
                    p = k * cols + other(col, d, cols)
                    arrival(obuf.at[p], o_recv.at[p]).wait_recv()
        for p in range(pieces):
            out_ref[:, p * cw:(p + 1) * cw] = obuf[p]

    @pl.when(lay == 0)
    def _():
        for p in range(pieces):
            for d in range(1, cols):
                first_copy(other(col, d, cols), p).wait_send()
                v_copy(other(col, d, cols), p).wait_send()

    for k in range(2):
        for d in range(cols):
            if k or d:
                y = other(col, d, cols)
                s_copy(k, y).wait_send()

                @pl.when(lay > 0)
                def _():
                    for h in range(cols):
                        u_copy(k, y, h).wait_send()
    for step in range(chunks):
        for h in range(cols):
            d_copy(step, h)[1].wait_send()

    def sums_sent(l, m, k):
        q = jnp.where(l == last, 2, k)
        same = plane(l) == plane(lay)
        for d in range(cols):
            c = other(col, d, cols)
            for b in range(ratio):
                for h in range(cols):
                    goal, copy = f_copy(q, c, b, h)
                    sent = goal != row
                    if d == 0:
                        sent = sent & jnp.logical_not(same)

                    @pl.when(sent)
                    def _():
                        copy.wait_send()

        if k == 0:
            @pl.when(l < last)
            def _():
                for d in range(1, cols):
                    for h in range(cols):
                        n_copy(k, m, other(col, d, cols), h).wait_send()

    def stage_sent(l, carry):
        m = jnp.where(l < last, l + 1, last - 1)
        for k in range(2):
            @pl.when(lay == holder(m, k))
            def _():
                sums_sent(l, m, k)

                @pl.when(l == last)
                def _():
                    spread_sent(2, incp.at[2], gup, 1, k, last)

            @pl.when(lay == holder(l, k))
            def _():
                spread_sent(k, incp.at[k], ginc, 0, k, l)

                @pl.when(l > 0)
                def _():
                    spread_sent(3 + k, natu.at[k], gup, 1, k, l - 1)
                    for c in range(cols):
                        @pl.when(jnp.logical_not((k == 0) & (col == c)))
                        def _():
                            o_copy(k, l, c).wait_send()

        return carry

    lax.fori_loop(0, layers, stage_sent, 0)


def per_device(layers, rows, cols, sources, transmission, reflection):
    ratio = rows // cols
    own, width = sources.shape[1], sources.shape[2]
    pieces = 2 * cols
    if layers % 2 or layers < 4 or rows % cols or width % (pieces * 128) or width // pieces % 3:
        return plain_per_device(layers, rows, cols, sources, transmission, reflection)
    part = -(-own // 16) * 16
    cw = width // pieces
    chunks = ratio * pieces
    r_tile = 256 if cw % 256 == 0 else 128
    traces = cols * part
    src = jnp.pad(sources[0], ((0, part - own), (0, 0)))
    dma, vmem = pltpu.SemaphoreType.DMA, pltpu.VMEM
    result = pl.pallas_call(
        functools.partial(kernel, layers, rows, cols, r_tile),
        out_shape=jax.ShapeDtypeStruct((part, width), BF16),
        in_specs=[
            pl.BlockSpec(memory_space=pltpu.VMEM),
            pl.BlockSpec(memory_space=pl.ANY),
            pl.BlockSpec(memory_space=pl.ANY),
        ],
        out_specs=pl.BlockSpec(memory_space=pltpu.VMEM),
        scratch_shapes=[
            vmem((chunks, width, cw), BF16),
            vmem((2, width, cw), BF16),
            vmem((pieces, part, cw), BF16),
            vmem((2, cols, part, cw), BF16),
            vmem((pieces, cols, part, cw), BF16),
            vmem((chunks, cols, part, cw), BF16),
            vmem((3, cols, ratio, cols, part, cw), BF16),
            vmem((3, rows, cols, part, cw), BF16),
            vmem((3, cols, part, cw), BF16),
            vmem((ratio, pieces, cols, part, cw), BF16),
            vmem((ratio, pieces, cols, part, cw), BF16),
            vmem((width // r_tile, traces, r_tile), F32),
            vmem((pieces, cols, part, cw), BF16),
            vmem((2, cols, cols, part, cw), BF16),
            vmem((2, cols, part, cw), BF16),
            vmem((pieces, part, cw), BF16),
            vmem((cols, pieces, part, cw), BF16),
            vmem((width // r_tile // 3, r_tile, traces), F32),
            dma((chunks,)), dma((2,)),
            dma((2, cols)), dma((2, cols)),
            dma((cols, pieces)), dma((cols, pieces)),
            dma((chunks, cols)), dma((3, cols, ratio, cols)),
            dma((3, cols, ratio, cols)), dma((3, rows, cols)),
            dma((2, cols, cols)), dma((pieces, cols)),
            dma((5, rows, cols)), dma((2, ratio, pieces, cols)),
            dma((pieces, cols)), dma((2, cols, cols)), dma((2, cols)), dma((pieces,)),
            dma((cols, pieces)), dma((cols, pieces)), pltpu.SemaphoreType.REGULAR,
        ],
        compiler_params=pltpu.CompilerParams(
            collective_id=0, has_side_effects=True, vmem_limit_bytes=66_000_000
        ),
    )(src, transmission[0], reflection[0])
    return result[None, :own]


def plain_kernel(
    layers, rows, cols, pieces, r_tile,
    src_ref, trans_ref, refl_ref, out_ref,
    tv, rbuf, sall, nin, incn, pbuf, ybuf, zbuf, natd, natu, ginc, gup, acc, ubuf, urec,
    t_sem, r_sem, s_send, s_recv, n_send, n_recv, y_send, y_recv, z_send, z_recv,
    g_send, g_recv, u_send, u_recv, go_sem,
):
    ratio = rows // cols
    chunks = ratio * pieces
    lay, row, col = (lax.axis_index(name) for name in ("layer", "row", "col"))
    part, cw = natd.shape[1], natd.shape[2]
    traces = cols * part
    tiles = acc.shape[0]
    last = layers - 1
    home_col, home_b = lax.div(row, ratio), lax.rem(row, ratio)

    def other(index, by, size):
        return lax.rem(index + by, size)

    def remote(src, dst, send, recv, target):
        return pltpu.make_async_remote_copy(
            src_ref=src, dst_ref=dst, send_sem=send, recv_sem=recv,
            device_id=target, device_id_type=MESH,
        )

    def column_block(step):
        return lax.rem(step, ratio) * pieces + lax.div(step, ratio)

    def t_copy(j):
        start = pl.multiple_of(j * cw, 128)
        return pltpu.make_async_copy(trans_ref.at[:, pl.ds(start, cw)], tv.at[j], t_sem.at[j])

    def r_copy(step):
        start = pl.multiple_of(column_block(step) * cw, 128)
        slot = lax.rem(step, 2)
        return pltpu.make_async_copy(
            refl_ref.at[:, pl.ds(start, cw)], rbuf.at[slot], r_sem.at[slot]
        )

    def copy_src(c):
        return remote(sall.at[col], sall.at[col], s_send.at[c], s_recv.at[col], (lay, row, c))

    def got_src(c):
        return remote(sall.at[c], sall.at[c], s_send.at[c], s_recv.at[c], (lay, row, c))

    def copy_next(c, p):
        return remote(natd.at[p], nin.at[col, p], n_send.at[c, p], n_recv.at[col, p],
                      (lax.min(lay + 1, last), row, c))

    def got_next(c, p):
        return remote(natd.at[p], nin.at[c, p], n_send.at[c, p], n_recv.at[c, p],
                      (lax.max(lay - 1, 0), row, c))

    def copy_y(c, j):
        return remote(pbuf.at[j, c], ybuf.at[col, j], y_send.at[c, j], y_recv.at[col, j],
                      (lay, row, c))

    def got_y(c, j):
        return remote(pbuf.at[j, c], ybuf.at[c, j], y_send.at[c, j], y_recv.at[c, j],
                      (lay, row, c))

    def copy_z(c, j, own):
        block = pbuf.at[j, col] if own else ybuf.at[c, j]
        goal = ratio * c + lax.div(j, pieces)
        return goal, block, remote(
            block, zbuf.at[row, lax.rem(j, pieces)], z_send.at[c, j],
            z_recv.at[row, lax.rem(j, pieces)], (lay, goal, col),
        )

    def got_z(r, p):
        return remote(natd.at[p], zbuf.at[r, p], z_send.at[0, 0], z_recv.at[r, p],
                      (lay, r, col))

    def copy_g(which, p, r):
        block = incn.at[p, col] if which == 0 else (natd, natu)[which - 1].at[p]
        buf, slot = (ginc, 0) if which == 0 else (gup, 1)
        target = lax.max(lay - 1, 0) if which == 2 else lay
        return block, buf, remote(
            block, buf.at[home_b, p, col], g_send.at[which, p, r],
            g_recv.at[slot, p, home_b, col], (target, r, home_col),
        )

    def got_g(slot, p, b, c):
        buf = gup if slot else ginc
        return remote(natd.at[p], buf.at[b, p, c], g_send.at[0, 0, 0],
                      g_recv.at[slot, p, b, c], (lay, ratio * col + b, c))

    def send_g(which, p):
        for d in range(1, rows):
            copy_g(which, p, other(row, d, rows))[2].start()
        block, buf, copy = copy_g(which, p, row)
        if which == 2:
            copy.start()
            return

        @pl.when(home_col == col)
        def _():
            buf[home_b, p, col] = block[...]

        @pl.when(home_col != col)
        def _():
            copy.start()

    def sent_g(which, p):
        for d in range(1, rows):
            copy_g(which, p, other(row, d, rows))[2].wait_send()
        copy = copy_g(which, p, row)[2]
        if which == 2:
            copy.wait_send()
            return

        @pl.when(home_col != col)
        def _():
            copy.wait_send()

    def arrived_g(slot, p, b):
        for c in range(cols):
            mine = (ratio * col + b == row) & (col == c)
            if slot:
                mine = mine & (lay == last)

            @pl.when(jnp.logical_not(mine))
            def _():
                got_g(slot, p, b, c).wait_recv()

    def copy_u(c, p):
        return remote(ubuf.at[c, p], urec.at[col, p], u_send.at[c, p], u_recv.at[col, p],
                      (lay, row, c))

    def got_u(c, p):
        return remote(ubuf.at[c, p], urec.at[c, p], u_send.at[c, p], u_recv.at[c, p],
                      (lay, row, c))

    for step in range(chunks):
        t_copy((step % ratio) * pieces + step // ratio).start()

    barrier = pltpu.get_barrier_semaphore()

    def greet(target):
        pl.semaphore_signal(barrier, inc=1, device_id=target, device_id_type=MESH)

    for dr in range(rows):
        for dc in range(cols):
            if dr or dc:
                greet((lay, other(row, dr, rows), other(col, dc, cols)))

    @pl.when(lay > 0)
    def _():
        for r in range(rows):
            for c in range(cols):
                greet((lay - 1, r, c))

    @pl.when(lay < last)
    def _():
        for r in range(rows):
            for c in range(cols):
                greet((lay + 1, r, c))

    near = (lay > 0).astype(jnp.int32) + (lay < last).astype(jnp.int32)
    pl.semaphore_wait(barrier, rows * cols - 1 + rows * cols * near)

    for p in range(pieces):
        sall[col, p] = src_ref[:, p * cw:(p + 1) * cw]
    for d in range(1, cols):
        copy_src(other(col, d, cols)).start()
    for step in range(2):
        r_copy(step).start()
    acc[...] = jnp.zeros_like(acc)
    for d in range(1, cols):
        got_src(other(col, d, cols)).wait_recv()

    @pl.when(lay == 0)
    def _():
        for p in range(pieces):
            incn[p] = sall[:, p]

    @pl.when(lay > 0)
    def _():
        for p in range(pieces):
            for c in range(cols):
                got_next(c, p).wait_recv()
            incn[p] = (nin[:, p].astype(F32) + sall[:, p].astype(F32)).astype(BF16)

    def to_row(c, j, own):
        goal, block, copy = copy_z(c, j, own)

        @pl.when(goal == row)
        def _():
            zbuf[row, lax.rem(j, pieces)] = block[...]

        @pl.when(goal != row)
        def _():
            copy.start()

    def forward(j):
        for d in range(1, cols):
            c = other(col, d, cols)
            got_y(c, j).wait_recv()
            to_row(c, j, False)

    def down_step(step, carry):
        j = column_block(step)
        t_copy(j).wait()
        total = jnp.zeros((traces, cw), F32)
        for p in range(pieces):
            total += jnp.dot(
                incn[p].reshape(traces, cw), tv[j, pl.ds(p * cw, cw), :],
                preferred_element_type=F32,
            )
        pbuf[j] = total.astype(BF16).reshape(cols, part, cw)
        for d in range(1, cols):
            copy_y(other(col, d, cols), j).start()
        to_row(col, j, True)

        @pl.when(step > 0)
        def _():
            forward(column_block(step - 1))

        return carry

    lax.fori_loop(0, chunks, down_step, 0)
    forward(column_block(chunks - 1))

    @pl.when(lay == last)
    def _():
        for p in range(pieces):
            send_g(0, p)

    for p in range(pieces):
        for d in range(1, rows):
            got_z(other(row, d, rows), p).wait_recv()
        natd[p] = jnp.sum(zbuf[:, p].astype(F32), axis=0).astype(BF16)

        @pl.when(lay < last)
        def _():
            for c in range(cols):
                copy_next(c, p).start()

        @pl.when(lay == last)
        def _():
            send_g(1, p)

    def signal_go():
        pl.semaphore_signal(
            go_sem, inc=1, device_id=(lay - 1, row, col), device_id_type=MESH
        )

    @pl.when((lay > 0) & (lay < last))
    def _():
        signal_go()

    @pl.when(lay < last)
    def _():
        early = pieces // 2
        for p in range(early):
            send_g(0, p)
        pl.semaphore_wait(go_sem, 1)
        for p in range(early, pieces):
            send_g(0, p)

    contract = (((1,), (1,)), ((), ()))

    def times(lhs, rhs):
        return lax.dot_general(lhs, rhs, contract, preferred_element_type=F32)

    def add_product(lhs, weights):
        for i in range(tiles):
            acc[i] += times(lhs, weights[pl.ds(i * r_tile, r_tile), :])

    def reflect_step(step, carry):
        b, p = lax.rem(step, ratio), lax.div(step, ratio)
        arrived_g(0, p, b)
        r_copy(step).wait()
        add_product(ginc[b, p].reshape(traces, cw), rbuf.at[lax.rem(step, 2)])

        @pl.when(step + 2 < chunks)
        def _():
            r_copy(step + 2).start()

        return carry

    lax.fori_loop(0, chunks, reflect_step, 0)

    def up_step(step, carry):
        b, p = lax.rem(step, ratio), lax.div(step, ratio)
        arrived_g(1, p, b)
        add_product(gup[b, p].reshape(traces, cw), tv.at[b * pieces + p])
        return carry

    lax.fori_loop(0, chunks - ratio, up_step, 0)
    end = pieces - 1
    for b in range(ratio):
        arrived_g(1, end, b)

    @pl.when((lay > 0) & (lay == last))
    def _():
        signal_go()

    per = cw // r_tile

    def piece_of(p, c):
        found = []
        for i in range(per):
            found.append(acc[p * per + i, pl.ds(pl.multiple_of(c * part, 8), part), :])
        return jnp.concatenate(found, axis=1)

    for p in range(pieces):
        for i in range(p * per, (p + 1) * per):
            total = acc[i]
            for b in range(ratio):
                total += times(
                    gup[b, end].reshape(traces, cw),
                    tv[b * pieces + end, pl.ds(i * r_tile, r_tile), :],
                )
            acc[i] = total
        for d in range(1, cols):
            c = other(col, d, cols)
            ubuf[c, p] = piece_of(p, c).astype(BF16)
            copy_u(c, p).start()

    for p in range(pieces):
        total = piece_of(p, col)
        for d in range(1, cols):
            c = other(col, d, cols)
            got_u(c, p).wait_recv()
            total += urec[c, p].astype(F32)
        result = total.astype(BF16)
        natu[p] = result
        out_ref[:, p * cw:(p + 1) * cw] = result

        @pl.when(lay > 0)
        def _():
            send_g(2, p)

    for d in range(1, cols):
        c = other(col, d, cols)
        copy_src(c).wait_send()
        for p in range(pieces):
            copy_u(c, p).wait_send()
        for j in range(chunks):
            copy_y(c, j).wait_send()
    for d in range(cols):
        c = other(col, d, cols)
        for j in range(chunks):
            goal, _, copy = copy_z(c, j, d == 0)

            @pl.when(goal != row)
            def _():
                copy.wait_send()

    for p in range(pieces):
        sent_g(0, p)

        @pl.when(lay < last)
        def _():
            for c in range(cols):
                copy_next(c, p).wait_send()

        @pl.when(lay == last)
        def _():
            sent_g(1, p)

        @pl.when(lay > 0)
        def _():
            sent_g(2, p)


def split_of(width):
    for pieces in (4, 3, 2):
        if width % (pieces * 128) == 0:
            return pieces
    return 1


def plain_per_device(layers, rows, cols, sources, transmission, reflection):
    ratio = rows // cols
    own, width = sources.shape[1], sources.shape[2]
    part = -(-own // 16) * 16
    pieces = split_of(width)
    cw = width // pieces
    chunks = ratio * pieces
    r_tile = 256 if cw % 256 == 0 else 128
    traces = cols * part
    src = jnp.pad(sources[0], ((0, part - own), (0, 0)))
    dma, vmem = pltpu.SemaphoreType.DMA, pltpu.VMEM
    result = pl.pallas_call(
        functools.partial(plain_kernel, layers, rows, cols, pieces, r_tile),
        out_shape=jax.ShapeDtypeStruct((part, width), BF16),
        in_specs=[
            pl.BlockSpec(memory_space=pltpu.VMEM),
            pl.BlockSpec(memory_space=pl.ANY),
            pl.BlockSpec(memory_space=pl.ANY),
        ],
        out_specs=pl.BlockSpec(memory_space=pltpu.VMEM),
        scratch_shapes=[
            vmem((chunks, width, cw), BF16),
            vmem((2, width, cw), BF16),
            vmem((cols, pieces, part, cw), BF16),
            vmem((cols, pieces, part, cw), BF16),
            vmem((pieces, cols, part, cw), BF16),
            vmem((chunks, cols, part, cw), BF16),
            vmem((cols, chunks, part, cw), BF16),
            vmem((rows, pieces, part, cw), BF16),
            vmem((pieces, part, cw), BF16),
            vmem((pieces, part, cw), BF16),
            vmem((ratio, pieces, cols, part, cw), BF16),
            vmem((ratio, pieces, cols, part, cw), BF16),
            vmem((width // r_tile, traces, r_tile), F32),
            vmem((cols, pieces, part, cw), BF16),
            vmem((cols, pieces, part, cw), BF16),
            dma((chunks,)), dma((2,)),
            dma((cols,)), dma((cols,)),
            dma((cols, pieces)), dma((cols, pieces)),
            dma((cols, chunks)), dma((cols, chunks)),
            dma((cols, chunks)), dma((rows, pieces)),
            dma((3, pieces, rows)), dma((2, pieces, ratio, cols)),
            dma((cols, pieces)), dma((cols, pieces)),
            pltpu.SemaphoreType.REGULAR,
        ],
        compiler_params=pltpu.CompilerParams(
            collective_id=0, has_side_effects=True, vmem_limit_bytes=66_000_000
        ),
    )(src, transmission[0], reflection[0])
    return result[None, :own]


def solution(mesh):
    sizes = [mesh.shape[name] for name in ("layer", "row", "col")]
    return jax.shard_map(
        functools.partial(per_device, *sizes),
        mesh=mesh,
        in_specs=(P("layer", "col", "row"), P("layer", "row", "col"), P("layer", "row", "col")),
        out_specs=P("layer", "col", "row"),
        check_vma=False,
    )
```

```python
import functools

import jax
import jax.numpy as jnp
from jax import lax
from jax.experimental import pallas as pl
from jax.experimental.pallas import tpu as pltpu
from jax.sharding import PartitionSpec as P

MESH = pl.DeviceIdType.MESH
BF16 = jnp.bfloat16
F32 = jnp.float32


def kernel(
    layers, rows, cols, r_tile,
    src_ref, trans_ref, refl_ref, out_ref,
    tv, rbuf, ssend, sp, incn, pbuf, rel, zbuf, incp, ginc, gup, acc, ubuf, urec, natu, obuf, vrec, acct,
    t_sem, r_sem, s_send, s_recv, i_send, i_recv, d_send, rel_recv, f_send, z_recv,
    n_send, n_recv, g_send, g_recv, u_send, u_recv, o_send, o_recv, v_send, v_recv, go_sem,
):
    ratio = rows // cols
    half = layers // 2
    pieces = 2 * cols
    chunks = ratio * pieces
    lay, row, col = (lax.axis_index(name) for name in ("layer", "row", "col"))
    part, cw = pbuf.shape[2], pbuf.shape[3]
    traces = cols * part
    per = cw // r_tile
    last = layers - 1
    late = last - 2
    home_col, home_b = lax.div(row, ratio), lax.rem(row, ratio)

    def other(index, by, size):
        return lax.rem(index + by, size)

    def peer(layer):
        return lax.rem(layer + half, layers)

    def holder(layer, k):
        if isinstance(layer, int):
            return (layer + k * half) % layers
        return lax.rem(layer + k * half, layers)

    def plane(layer):
        return lax.div(layer, half)

    def remote(src, dst, send, recv, target):
        return pltpu.make_async_remote_copy(
            src_ref=src, dst_ref=dst, send_sem=send, recv_sem=recv,
            device_id=target, device_id_type=MESH,
        )

    me = (lay, row, col)
    up_peer = lax.rem(lay + 1, layers)

    def arrival(dst, recv):
        return remote(dst, dst, recv, recv, (up_peer, row, col))

    base = jnp.where(lay < last, lay + 1, last - 1)
    near_k = jnp.where(plane(base) == plane(lay), 0, 1)

    def order(step):
        near, o = lax.rem(step, 2), lax.div(step, 2 * ratio)
        b = lax.rem(lax.div(step, 2), ratio)
        d = cols - 1 - o
        k = jnp.where(near == 1, near_k, 1 - near_k)
        y = other(col, d, cols)
        return near, d, k, y, b, k * cols + y

    def t_copy(j):
        start = pl.multiple_of(j * cw, 128)
        return pltpu.make_async_copy(trans_ref.at[:, pl.ds(start, cw)], tv.at[j], t_sem.at[j])

    def r_index(step):
        p, b = lax.div(step, ratio), lax.rem(step, ratio)
        return b, p

    def r_copy(step):
        b, p = r_index(step)
        start = pl.multiple_of((b * pieces + p) * cw, 128)
        slot = lax.rem(step, 2)
        return pltpu.make_async_copy(
            refl_ref.at[:, pl.ds(start, cw)], rbuf.at[slot], r_sem.at[slot]
        )

    for step in range(chunks):
        b, p = order(step)[-2:]
        t_copy(b * pieces + p).start()

    barrier = pltpu.get_barrier_semaphore()
    for dl in range(layers):
        for dr in range(rows):
            for dc in range(cols):
                if dl or dr or dc:
                    pl.semaphore_signal(
                        barrier, inc=1, device_id_type=MESH,
                        device_id=(other(lay, dl, layers), other(row, dr, rows), other(col, dc, cols)),
                    )
    pl.semaphore_wait(barrier, layers * rows * cols - 1)

    for k in range(2):
        for y in range(cols):
            p = k * cols + y
            ssend[p] = src_ref[:, p * cw:(p + 1) * cw]

    def first_copy(c, p):
        return remote(ssend.at[p], incn.at[p, col], i_send.at[c, p], i_recv.at[col, p], (lay, row, c))

    @pl.when(lay == 0)
    def _():
        for p in range(pieces):
            for d in range(1, cols):
                first_copy(other(col, d, cols), p).start()
            incn[p, col] = ssend[p]

    def s_copy(k, y):
        return remote(ssend.at[k * cols + y], sp.at[k, col], s_send.at[k, y], s_recv.at[k, col],
                      (holder(lay, k), row, y))

    for k in (1, 0):
        for d in range(cols):
            if k or d:
                s_copy(k, other(col, d, cols)).start()
    sp[0, col] = ssend[col]
    acc[...] = jnp.zeros_like(acc)
    acct[...] = jnp.zeros_like(acct)

    def got_s(k):
        for d in range(cols):
            if k or d:
                c = other(col, d, cols)
                arrival(sp.at[k, c], s_recv.at[k, c]).wait_recv()

    def g_copy(slot, block, buf, which, k, layer, r, h):
        p = k * cols + col
        if which == 0:
            return remote(block, buf.at[home_b, p], g_send.at[slot, r, h],
                          g_recv.at[which, home_b, p, h], (layer, r, home_col))
        return remote(block.at[h], buf.at[home_b, p, h], g_send.at[slot, r, h],
                      g_recv.at[which, home_b, p, h], (layer, r, home_col))

    def spread_part(slot, block, buf, which, k, layer, h):
        for d in range(1, rows):
            g_copy(slot, block, buf, which, k, layer, other(row, d, rows), h).start()
        mine = (layer == lay) & (home_col == col)

        @pl.when(mine)
        def _():
            if which == 0:
                buf[home_b, k * cols + col] = block[...]
            else:
                buf[home_b, k * cols + col, h] = block[h]

        @pl.when(jnp.logical_not(mine))
        def _():
            g_copy(slot, block, buf, which, k, layer, row, h).start()

    def spread(slot, block, buf, which, k, layer):
        for h in range(cols if which else 1):
            spread_part(slot, block, buf, which, k, layer, h)

    def spread_sent(slot, block, buf, which, k, layer):
        for h in range(cols if which else 1):
            for d in range(1, rows):
                g_copy(slot, block, buf, which, k, layer, other(row, d, rows), h).wait_send()

            @pl.when(jnp.logical_not((layer == lay) & (home_col == col)))
            def _():
                g_copy(slot, block, buf, which, k, layer, row, h).wait_send()

    def arrived_g(which, b, p):
        buf = gup if which else ginc
        if which:
            for h in range(cols):
                arrival(buf.at[b, p, h], g_recv.at[which, b, p, h]).wait_recv()
            return
        mine = (ratio * col + b == row) & (p == col)

        @pl.when(jnp.logical_not(mine))
        def _():
            arrival(buf.at[b, p], g_recv.at[which, b, p, 0]).wait_recv()

    for k in range(2):
        @pl.when(lay == k * half)
        def _():
            got_s(k)
            incp[k] = sp[k]
            if k:
                spread(k, incp.at[k], ginc, 0, k, 0)

    def d_copy(step, h):
        near, d, k, y, b, p = order(step)
        j = b * pieces + p
        q = jnp.where(lay == last, 2, k)
        target = holder(base, k)
        direct = (near == 1) & (d == 0)
        return direct, remote(
            pbuf.at[j, h], zbuf.at[q, row, h], d_send.at[j, h], z_recv.at[q, row, h],
            (target, ratio * col + b, col),
        ), remote(
            pbuf.at[j, h], rel.at[q, col, b, h], d_send.at[j, h], rel_recv.at[q, col, b, h],
            (target, row, y),
        )

    def down_compute():
        @pl.when(lay == 0)
        def _():
            for p in range(pieces):
                for d in range(1, cols):
                    c = other(col, d, cols)
                    arrival(incn.at[p, c], i_recv.at[c, p]).wait_recv()
            spread(0, incp.at[0], ginc, 0, 0, 0)

        @pl.when(lay > 0)
        def _():
            for k in range(2):
                for d in range(cols):
                    if k or d:
                        p = k * cols + other(col, d, cols)
                        for h in range(cols):
                            arrival(incn.at[p, h], n_recv.at[p, h]).wait_recv()

            @pl.when(lay != late)
            def _():
                spread(0, incp.at[0], ginc, 0, 0, lay)

        def down_step(step, carry):
            b, p = order(step)[-2:]
            j = b * pieces + p
            t_copy(j).wait()
            total = jnp.zeros((traces, cw), F32)
            for i in range(pieces):
                total += jnp.dot(
                    incn[i].reshape(traces, cw), tv[j, pl.ds(i * cw, cw), :],
                    preferred_element_type=F32,
                )
            pbuf[j] = total.astype(BF16).reshape(cols, part, cw)
            for h in range(cols):
                direct, straight, relayed = d_copy(step, h)

                @pl.when(direct)
                def _():
                    straight.start()

                @pl.when(jnp.logical_not(direct))
                def _():
                    relayed.start()

            return carry

        lax.fori_loop(0, chunks, down_step, 0)
        for step in range(2):
            r_copy(step).start()

        tiles = acc.shape[0]

        def turn_step(step, carry):
            at, i = lax.div(step, tiles), lax.rem(step, tiles)
            j = lax.rem(at, ratio) * pieces + lax.div(at, ratio)
            rows_at = pl.ds(pl.multiple_of(i * r_tile, r_tile), r_tile)
            turned = [tv[j, rows_at, n * r_tile:(n + 1) * r_tile].T for n in range(per)]
            for n in range(per):
                tv[j, rows_at, n * r_tile:(n + 1) * r_tile] = turned[n]
            return carry

        turns = jnp.where(lay == last, cols, pieces) * (ratio * tiles)
        lax.fori_loop(0, turns, turn_step, 0)

    def f_copy(q, c, b, h):
        goal = ratio * c + b
        return goal, remote(rel.at[q, c, b, h], zbuf.at[q, row, h], f_send.at[q, c, b, h],
                            z_recv.at[q, row, h], (lay, goal, col))

    def n_copy(k, layer, c, h):
        p = k * cols + col
        return remote(incp.at[k, h], incn.at[p, h], n_send.at[k, c, h], n_recv.at[p, h],
                      (layer, row, c))

    def forward(q, c):
        for b in range(ratio):
            for h in range(cols):
                arrival(rel.at[q, c, b, h], rel_recv.at[q, c, b, h]).wait_recv()
                goal, copy = f_copy(q, c, b, h)

                @pl.when(goal == row)
                def _():
                    zbuf[q, row, h] = rel[q, c, b, h]

                @pl.when(goal != row)
                def _():
                    copy.start()

    def down_sum(l, m, k):
        q = jnp.where(l == last, 2, k)
        same = plane(l) == plane(lay)
        for d in range(1, cols):
            forward(q, other(col, d, cols))

        @pl.when(jnp.logical_not(same))
        def _():
            forward(q, col)

        for h in range(cols):
            for d in range(rows):
                r = other(row, d, rows)
                if d:
                    arrival(zbuf.at[q, r, h], z_recv.at[q, r, h]).wait_recv()
                else:
                    @pl.when(same & (home_col == col))
                    def _():
                        arrival(zbuf.at[q, r, h], z_recv.at[q, r, h]).wait_recv()

            down = jnp.sum(zbuf[q, :, h].astype(F32), axis=0).astype(BF16)

            @pl.when(l < last)
            def _():
                incp[k, h] = (down.astype(F32) + sp[k, h].astype(F32)).astype(BF16)
                for d in range(1, cols):
                    n_copy(k, m, other(col, d, cols), h).start()
                if k:
                    n_copy(k, m, col, h).start()
                else:
                    incn[col, h] = incp[k, h]

            @pl.when(l == last)
            def _():
                incp[2, h] = down
                spread_part(2, incp.at[2], gup, 1, k, last, h)

        if k == 1:
            @pl.when(l < last)
            def _():
                for c in range(cols):
                    for h in range(cols):
                        n_copy(k, m, c, h).wait_send()

                @pl.when(m != late)
                def _():
                    spread(k, incp.at[k], ginc, 0, k, m)

    contract = (((1,), (1,)), ((), ()))

    def times(lhs, rhs):
        return lax.dot_general(lhs, rhs, contract, preferred_element_type=F32)

    def add_products(lhs, weights):
        for i in range(acc.shape[0]):
            tile = weights[pl.ds(i * r_tile, r_tile), :]
            if i % 3 == 1:
                acct[i // 3] += times(tile, lhs)
            else:
                acc[i] += times(lhs, tile)

    def turn_products():
        for q in range(acct.shape[0]):
            acc[3 * q + 1] += acct[q].T

    def reflect():
        def reflect_step(step, carry):
            b, p = r_index(step)
            arrived_g(0, b, p)
            r_copy(step).wait()
            lhs = ginc[b, p].reshape(traces, cw)
            slot = lax.rem(step, 2)
            add_products(lhs, rbuf.at[slot])

            @pl.when(step + 2 < chunks)
            def _():
                r_copy(step + 2).start()

            return carry

        lax.fori_loop(0, chunks, reflect_step, 0)

        @pl.when(lay < last)
        def _():
            turn_products()

    def u_copy(k, y, h):
        p = k * cols + y
        return remote(ubuf.at[p, h], urec.at[k, col, h], u_send.at[p, h], u_recv.at[k, col, h],
                      (holder(lay, k), row, y))

    def times_turned(lhs, j, start):
        total = None
        for n in range(per):
            term = jnp.dot(
                lhs[:, n * r_tile:(n + 1) * r_tile],
                tv[j, pl.ds(start, r_tile), n * r_tile:(n + 1) * r_tile],
                preferred_element_type=F32,
            )
            total = term if total is None else total + term
        return total

    def v_copy(c, p):
        return remote(ubuf.at[p, c], vrec.at[col, p], v_send.at[c, p], v_recv.at[col, p],
                      (lay, row, c))

    def top_sum():
        mine = pl.ds(pl.multiple_of(col * part, 16), part)
        for p in list(range(cols, pieces)) + list(range(cols)):
            for d in range(1, cols):
                c = other(col, d, cols)
                arrival(vrec.at[c, p], v_recv.at[c, p]).wait_recv()
            for i in range(per):
                lanes = slice(i * r_tile, (i + 1) * r_tile)
                total = acc[p * per + i, mine, :]
                for d in range(1, cols):
                    total += vrec[other(col, d, cols), p, :, lanes].astype(F32)
                start = p * cw + i * r_tile
                out_ref[:, start:start + r_tile] = total.astype(BF16)

    def up_compute():
        def lead_step(step, carry):
            b, p = lax.rem(step, ratio), cols + lax.div(step, ratio)
            arrived_g(1, b, p)

            @pl.when((step == 0) & (lay == last))
            def _():
                for k in range(2):
                    target = holder(late, k)
                    if target == last:
                        spread(k, incp.at[k], ginc, 0, k, late)
                    else:
                        pl.semaphore_signal(
                            go_sem, inc=1, device_id=(target, row, col), device_id_type=MESH
                        )

            lhs = gup[b, p].reshape(traces, cw)
            j = b * pieces + p

            @pl.when(lay == last)
            def _():
                add_products(lhs, tv.at[j])

            @pl.when(lay < last)
            def _():
                for i in range(acc.shape[0]):
                    acc[i] += times_turned(lhs, j, i * r_tile)

            return carry

        lax.fori_loop(0, ratio * cols, lead_step, 0)

        @pl.when(lay == last)
        def _():
            turn_products()

        for p in range(cols):
            for b in range(ratio):
                arrived_g(1, b, p)

        def piece_step(o, carry):
            k = 1 - lax.div(o, cols)
            y = other(col, cols - 1 - lax.rem(o, cols), cols)
            p = k * cols + y
            for i in range(per):
                tile = p * per + i
                start = pl.multiple_of(tile * r_tile, r_tile)
                total = acc[tile]
                for pp in range(cols):
                    for b in range(ratio):
                        total += times_turned(
                            gup[b, pp].reshape(traces, cw), b * pieces + pp, start
                        )
                acc[tile] = total

            @pl.when((o < pieces - 1) | (lay == 0))
            def _():
                for i in range(per):
                    ubuf[p, :, :, i * r_tile:(i + 1) * r_tile] = (
                        acc[p * per + i].astype(BF16).reshape(cols, part, r_tile)
                    )

            @pl.when((o < pieces - 1) & (lay > 0))
            def _():
                for h in range(cols):
                    u_copy(k, y, h).start()

            @pl.when(lay == 0)
            def _():
                for d in range(1, cols):
                    v_copy(other(col, d, cols), p).start()

            return carry

        lax.fori_loop(0, pieces, piece_step, 0)

    def o_copy(k, layer, c):
        p = k * cols + col
        return remote(natu.at[k, c], obuf.at[p], o_send.at[k, c], o_recv.at[p], (layer, row, c))

    def up_sum(l, k):
        for h in range(cols):
            for d in range(cols):
                if k or d:
                    c = other(col, d, cols)
                    arrival(urec.at[k, c, h], u_recv.at[k, c, h]).wait_recv()
            if k == 0:
                for i in range(per):
                    lanes = slice(i * r_tile, (i + 1) * r_tile)
                    total = acc[col * per + i, h * part:(h + 1) * part]
                    for d in range(1, cols):
                        total += urec[0, other(col, d, cols), h, :, lanes].astype(F32)
                    natu[0, h, :, lanes] = total.astype(BF16)
            else:
                natu[1, h] = jnp.sum(urec[1, :, h].astype(F32), axis=0).astype(BF16)

            spread_part(3 + k, natu.at[k], gup, 1, k, l - 1, h)

        for c in range(cols):
            mine = (k == 0) & (col == c)

            @pl.when(mine)
            def _():
                obuf[k * cols + col] = natu[k, c]

            @pl.when(jnp.logical_not(mine))
            def _():
                o_copy(k, l, c).start()

    def stage(t, carry):
        down = t < layers
        l = jnp.where(down, t, 2 * layers - 1 - t)

        @pl.when(down & (lay == l))
        def _():
            down_compute()

        m = jnp.where(l < last, l + 1, last - 1)
        for k in range(2):
            @pl.when(down & (lay == holder(m, k)))
            def _():
                @pl.when(l < last)
                def _():
                    got_s(k)

                down_sum(l, m, k)

        for k in range(2):
            @pl.when((t == layers) & (lay == holder(late, k)) & (lay != last))
            def _():
                pl.semaphore_wait(go_sem, 1)
                spread(k, incp.at[k], ginc, 0, k, late)

        @pl.when(t == jnp.where(lay == late, layers + 1, lax.min(lay + 2, layers)))
        def _():
            reflect()

        @pl.when(jnp.logical_not(down) & (lay == l))
        def _():
            up_compute()

        for k in range(2):
            @pl.when(jnp.logical_not(down) & (l > 0) & (lay == holder(l, k)))
            def _():
                up_sum(l, k)

        return carry

    lax.fori_loop(0, 2 * layers, stage, 0)

    @pl.when(lay == 0)
    def _():
        top_sum()

    @pl.when(lay > 0)
    def _():
        for k in range(2):
            for d in range(cols):
                if k or d:
                    p = k * cols + other(col, d, cols)
                    arrival(obuf.at[p], o_recv.at[p]).wait_recv()
        for p in range(pieces):
            out_ref[:, p * cw:(p + 1) * cw] = obuf[p]

    @pl.when(lay == 0)
    def _():
        for p in range(pieces):
            for d in range(1, cols):
                first_copy(other(col, d, cols), p).wait_send()
                v_copy(other(col, d, cols), p).wait_send()

    for k in range(2):
        for d in range(cols):
            if k or d:
                y = other(col, d, cols)
                s_copy(k, y).wait_send()

                @pl.when(lay > 0)
                def _():
                    for h in range(cols):
                        u_copy(k, y, h).wait_send()
    for step in range(chunks):
        for h in range(cols):
            d_copy(step, h)[1].wait_send()

    def sums_sent(l, m, k):
        q = jnp.where(l == last, 2, k)
        same = plane(l) == plane(lay)
        for d in range(cols):
            c = other(col, d, cols)
            for b in range(ratio):
                for h in range(cols):
                    goal, copy = f_copy(q, c, b, h)
                    sent = goal != row
                    if d == 0:
                        sent = sent & jnp.logical_not(same)

                    @pl.when(sent)
                    def _():
                        copy.wait_send()

        if k == 0:
            @pl.when(l < last)
            def _():
                for d in range(1, cols):
                    for h in range(cols):
                        n_copy(k, m, other(col, d, cols), h).wait_send()

    def stage_sent(l, carry):
        m = jnp.where(l < last, l + 1, last - 1)
        for k in range(2):
            @pl.when(lay == holder(m, k))
            def _():
                sums_sent(l, m, k)

                @pl.when(l == last)
                def _():
                    spread_sent(2, incp.at[2], gup, 1, k, last)

            @pl.when(lay == holder(l, k))
            def _():
                spread_sent(k, incp.at[k], ginc, 0, k, l)

                @pl.when(l > 0)
                def _():
                    spread_sent(3 + k, natu.at[k], gup, 1, k, l - 1)
                    for c in range(cols):
                        @pl.when(jnp.logical_not((k == 0) & (col == c)))
                        def _():
                            o_copy(k, l, c).wait_send()

        return carry

    lax.fori_loop(0, layers, stage_sent, 0)


def per_device(layers, rows, cols, sources, transmission, reflection):
    ratio = rows // cols
    own, width = sources.shape[1], sources.shape[2]
    pieces = 2 * cols
    if layers % 2 or layers < 4 or rows % cols or width % (pieces * 128) or width // pieces % 3:
        return plain_per_device(layers, rows, cols, sources, transmission, reflection)
    part = -(-own // 16) * 16
    cw = width // pieces
    chunks = ratio * pieces
    r_tile = 256 if cw % 256 == 0 else 128
    traces = cols * part
    src = jnp.pad(sources[0], ((0, part - own), (0, 0)))
    dma, vmem = pltpu.SemaphoreType.DMA, pltpu.VMEM
    result = pl.pallas_call(
        functools.partial(kernel, layers, rows, cols, r_tile),
        out_shape=jax.ShapeDtypeStruct((part, width), BF16),
        in_specs=[
            pl.BlockSpec(memory_space=pltpu.VMEM),
            pl.BlockSpec(memory_space=pl.ANY),
            pl.BlockSpec(memory_space=pl.ANY),
        ],
        out_specs=pl.BlockSpec(memory_space=pltpu.VMEM),
        scratch_shapes=[
            vmem((chunks, width, cw), BF16),
            vmem((2, width, cw), BF16),
            vmem((pieces, part, cw), BF16),
            vmem((2, cols, part, cw), BF16),
            vmem((pieces, cols, part, cw), BF16),
            vmem((chunks, cols, part, cw), BF16),
            vmem((3, cols, ratio, cols, part, cw), BF16),
            vmem((3, rows, cols, part, cw), BF16),
            vmem((3, cols, part, cw), BF16),
            vmem((ratio, pieces, cols, part, cw), BF16),
            vmem((ratio, pieces, cols, part, cw), BF16),
            vmem((width // r_tile, traces, r_tile), F32),
            vmem((pieces, cols, part, cw), BF16),
            vmem((2, cols, cols, part, cw), BF16),
            vmem((2, cols, part, cw), BF16),
            vmem((pieces, part, cw), BF16),
            vmem((cols, pieces, part, cw), BF16),
            vmem((width // r_tile // 3, r_tile, traces), F32),
            dma((chunks,)), dma((2,)),
            dma((2, cols)), dma((2, cols)),
            dma((cols, pieces)), dma((cols, pieces)),
            dma((chunks, cols)), dma((3, cols, ratio, cols)),
            dma((3, cols, ratio, cols)), dma((3, rows, cols)),
            dma((2, cols, cols)), dma((pieces, cols)),
            dma((5, rows, cols)), dma((2, ratio, pieces, cols)),
            dma((pieces, cols)), dma((2, cols, cols)), dma((2, cols)), dma((pieces,)),
            dma((cols, pieces)), dma((cols, pieces)), pltpu.SemaphoreType.REGULAR,
        ],
        compiler_params=pltpu.CompilerParams(
            collective_id=0, has_side_effects=True, vmem_limit_bytes=66_000_000
        ),
    )(src, transmission[0], reflection[0])
    return result[None, :own]


def plain_kernel(
    layers, rows, cols, pieces, r_tile,
    src_ref, trans_ref, refl_ref, out_ref,
    tv, rbuf, sall, nin, incn, pbuf, ybuf, zbuf, natd, natu, ginc, gup, acc, ubuf, urec,
    t_sem, r_sem, s_send, s_recv, n_send, n_recv, y_send, y_recv, z_send, z_recv,
    g_send, g_recv, u_send, u_recv, go_sem,
):
    ratio = rows // cols
    chunks = ratio * pieces
    lay, row, col = (lax.axis_index(name) for name in ("layer", "row", "col"))
    part, cw = natd.shape[1], natd.shape[2]
    traces = cols * part
    tiles = acc.shape[0]
    last = layers - 1
    home_col, home_b = lax.div(row, ratio), lax.rem(row, ratio)

    def other(index, by, size):
        return lax.rem(index + by, size)

    def remote(src, dst, send, recv, target):
        return pltpu.make_async_remote_copy(
            src_ref=src, dst_ref=dst, send_sem=send, recv_sem=recv,
            device_id=target, device_id_type=MESH,
        )

    def column_block(step):
        return lax.rem(step, ratio) * pieces + lax.div(step, ratio)

    def t_copy(j):
        start = pl.multiple_of(j * cw, 128)
        return pltpu.make_async_copy(trans_ref.at[:, pl.ds(start, cw)], tv.at[j], t_sem.at[j])

    def r_copy(step):
        start = pl.multiple_of(column_block(step) * cw, 128)
        slot = lax.rem(step, 2)
        return pltpu.make_async_copy(
            refl_ref.at[:, pl.ds(start, cw)], rbuf.at[slot], r_sem.at[slot]
        )

    def copy_src(c):
        return remote(sall.at[col], sall.at[col], s_send.at[c], s_recv.at[col], (lay, row, c))

    def got_src(c):
        return remote(sall.at[c], sall.at[c], s_send.at[c], s_recv.at[c], (lay, row, c))

    def copy_next(c, p):
        return remote(natd.at[p], nin.at[col, p], n_send.at[c, p], n_recv.at[col, p],
                      (lax.min(lay + 1, last), row, c))

    def got_next(c, p):
        return remote(natd.at[p], nin.at[c, p], n_send.at[c, p], n_recv.at[c, p],
                      (lax.max(lay - 1, 0), row, c))

    def copy_y(c, j):
        return remote(pbuf.at[j, c], ybuf.at[col, j], y_send.at[c, j], y_recv.at[col, j],
                      (lay, row, c))

    def got_y(c, j):
        return remote(pbuf.at[j, c], ybuf.at[c, j], y_send.at[c, j], y_recv.at[c, j],
                      (lay, row, c))

    def copy_z(c, j, own):
        block = pbuf.at[j, col] if own else ybuf.at[c, j]
        goal = ratio * c + lax.div(j, pieces)
        return goal, block, remote(
            block, zbuf.at[row, lax.rem(j, pieces)], z_send.at[c, j],
            z_recv.at[row, lax.rem(j, pieces)], (lay, goal, col),
        )

    def got_z(r, p):
        return remote(natd.at[p], zbuf.at[r, p], z_send.at[0, 0], z_recv.at[r, p],
                      (lay, r, col))

    def copy_g(which, p, r):
        block = incn.at[p, col] if which == 0 else (natd, natu)[which - 1].at[p]
        buf, slot = (ginc, 0) if which == 0 else (gup, 1)
        target = lax.max(lay - 1, 0) if which == 2 else lay
        return block, buf, remote(
            block, buf.at[home_b, p, col], g_send.at[which, p, r],
            g_recv.at[slot, p, home_b, col], (target, r, home_col),
        )

    def got_g(slot, p, b, c):
        buf = gup if slot else ginc
        return remote(natd.at[p], buf.at[b, p, c], g_send.at[0, 0, 0],
                      g_recv.at[slot, p, b, c], (lay, ratio * col + b, c))

    def send_g(which, p):
        for d in range(1, rows):
            copy_g(which, p, other(row, d, rows))[2].start()
        block, buf, copy = copy_g(which, p, row)
        if which == 2:
            copy.start()
            return

        @pl.when(home_col == col)
        def _():
            buf[home_b, p, col] = block[...]

        @pl.when(home_col != col)
        def _():
            copy.start()

    def sent_g(which, p):
        for d in range(1, rows):
            copy_g(which, p, other(row, d, rows))[2].wait_send()
        copy = copy_g(which, p, row)[2]
        if which == 2:
            copy.wait_send()
            return

        @pl.when(home_col != col)
        def _():
            copy.wait_send()

    def arrived_g(slot, p, b):
        for c in range(cols):
            mine = (ratio * col + b == row) & (col == c)
            if slot:
                mine = mine & (lay == last)

            @pl.when(jnp.logical_not(mine))
            def _():
                got_g(slot, p, b, c).wait_recv()

    def copy_u(c, p):
        return remote(ubuf.at[c, p], urec.at[col, p], u_send.at[c, p], u_recv.at[col, p],
                      (lay, row, c))

    def got_u(c, p):
        return remote(ubuf.at[c, p], urec.at[c, p], u_send.at[c, p], u_recv.at[c, p],
                      (lay, row, c))

    for step in range(chunks):
        t_copy((step % ratio) * pieces + step // ratio).start()

    barrier = pltpu.get_barrier_semaphore()

    def greet(target):
        pl.semaphore_signal(barrier, inc=1, device_id=target, device_id_type=MESH)

    for dr in range(rows):
        for dc in range(cols):
            if dr or dc:
                greet((lay, other(row, dr, rows), other(col, dc, cols)))

    @pl.when(lay > 0)
    def _():
        for r in range(rows):
            for c in range(cols):
                greet((lay - 1, r, c))

    @pl.when(lay < last)
    def _():
        for r in range(rows):
            for c in range(cols):
                greet((lay + 1, r, c))

    near = (lay > 0).astype(jnp.int32) + (lay < last).astype(jnp.int32)
    pl.semaphore_wait(barrier, rows * cols - 1 + rows * cols * near)

    for p in range(pieces):
        sall[col, p] = src_ref[:, p * cw:(p + 1) * cw]
    for d in range(1, cols):
        copy_src(other(col, d, cols)).start()
    for step in range(2):
        r_copy(step).start()
    acc[...] = jnp.zeros_like(acc)
    for d in range(1, cols):
        got_src(other(col, d, cols)).wait_recv()

    @pl.when(lay == 0)
    def _():
        for p in range(pieces):
            incn[p] = sall[:, p]

    @pl.when(lay > 0)
    def _():
        for p in range(pieces):
            for c in range(cols):
                got_next(c, p).wait_recv()
            incn[p] = (nin[:, p].astype(F32) + sall[:, p].astype(F32)).astype(BF16)

    def to_row(c, j, own):
        goal, block, copy = copy_z(c, j, own)

        @pl.when(goal == row)
        def _():
            zbuf[row, lax.rem(j, pieces)] = block[...]

        @pl.when(goal != row)
        def _():
            copy.start()

    def forward(j):
        for d in range(1, cols):
            c = other(col, d, cols)
            got_y(c, j).wait_recv()
            to_row(c, j, False)

    def down_step(step, carry):
        j = column_block(step)
        t_copy(j).wait()
        total = jnp.zeros((traces, cw), F32)
        for p in range(pieces):
            total += jnp.dot(
                incn[p].reshape(traces, cw), tv[j, pl.ds(p * cw, cw), :],
                preferred_element_type=F32,
            )
        pbuf[j] = total.astype(BF16).reshape(cols, part, cw)
        for d in range(1, cols):
            copy_y(other(col, d, cols), j).start()
        to_row(col, j, True)

        @pl.when(step > 0)
        def _():
            forward(column_block(step - 1))

        return carry

    lax.fori_loop(0, chunks, down_step, 0)
    forward(column_block(chunks - 1))

    @pl.when(lay == last)
    def _():
        for p in range(pieces):
            send_g(0, p)

    for p in range(pieces):
        for d in range(1, rows):
            got_z(other(row, d, rows), p).wait_recv()
        natd[p] = jnp.sum(zbuf[:, p].astype(F32), axis=0).astype(BF16)

        @pl.when(lay < last)
        def _():
            for c in range(cols):
                copy_next(c, p).start()

        @pl.when(lay == last)
        def _():
            send_g(1, p)

    def signal_go():
        pl.semaphore_signal(
            go_sem, inc=1, device_id=(lay - 1, row, col), device_id_type=MESH
        )

    @pl.when((lay > 0) & (lay < last))
    def _():
        signal_go()

    @pl.when(lay < last)
    def _():
        early = pieces // 2
        for p in range(early):
            send_g(0, p)
        pl.semaphore_wait(go_sem, 1)
        for p in range(early, pieces):
            send_g(0, p)

    contract = (((1,), (1,)), ((), ()))

    def times(lhs, rhs):
        return lax.dot_general(lhs, rhs, contract, preferred_element_type=F32)

    def add_product(lhs, weights):
        for i in range(tiles):
            acc[i] += times(lhs, weights[pl.ds(i * r_tile, r_tile), :])

    def reflect_step(step, carry):
        b, p = lax.rem(step, ratio), lax.div(step, ratio)
        arrived_g(0, p, b)
        r_copy(step).wait()
        add_product(ginc[b, p].reshape(traces, cw), rbuf.at[lax.rem(step, 2)])

        @pl.when(step + 2 < chunks)
        def _():
            r_copy(step + 2).start()

        return carry

    lax.fori_loop(0, chunks, reflect_step, 0)

    def up_step(step, carry):
        b, p = lax.rem(step, ratio), lax.div(step, ratio)
        arrived_g(1, p, b)
        add_product(gup[b, p].reshape(traces, cw), tv.at[b * pieces + p])
        return carry

    lax.fori_loop(0, chunks - ratio, up_step, 0)
    end = pieces - 1
    for b in range(ratio):
        arrived_g(1, end, b)

    @pl.when((lay > 0) & (lay == last))
    def _():
        signal_go()

    per = cw // r_tile

    def piece_of(p, c):
        found = []
        for i in range(per):
            found.append(acc[p * per + i, pl.ds(pl.multiple_of(c * part, 8), part), :])
        return jnp.concatenate(found, axis=1)

    for p in range(pieces):
        for i in range(p * per, (p + 1) * per):
            total = acc[i]
            for b in range(ratio):
                total += times(
                    gup[b, end].reshape(traces, cw),
                    tv[b * pieces + end, pl.ds(i * r_tile, r_tile), :],
                )
            acc[i] = total
        for d in range(1, cols):
            c = other(col, d, cols)
            ubuf[c, p] = piece_of(p, c).astype(BF16)
            copy_u(c, p).start()

    for p in range(pieces):
        total = piece_of(p, col)
        for d in range(1, cols):
            c = other(col, d, cols)
            got_u(c, p).wait_recv()
            total += urec[c, p].astype(F32)
        result = total.astype(BF16)
        natu[p] = result
        out_ref[:, p * cw:(p + 1) * cw] = result

        @pl.when(lay > 0)
        def _():
            send_g(2, p)

    for d in range(1, cols):
        c = other(col, d, cols)
        copy_src(c).wait_send()
        for p in range(pieces):
            copy_u(c, p).wait_send()
        for j in range(chunks):
            copy_y(c, j).wait_send()
    for d in range(cols):
        c = other(col, d, cols)
        for j in range(chunks):
            goal, _, copy = copy_z(c, j, d == 0)

            @pl.when(goal != row)
            def _():
                copy.wait_send()

    for p in range(pieces):
        sent_g(0, p)

        @pl.when(lay < last)
        def _():
            for c in range(cols):
                copy_next(c, p).wait_send()

        @pl.when(lay == last)
        def _():
            sent_g(1, p)

        @pl.when(lay > 0)
        def _():
            sent_g(2, p)


def split_of(width):
    for pieces in (4, 3, 2):
        if width % (pieces * 128) == 0:
            return pieces
    return 1


def plain_per_device(layers, rows, cols, sources, transmission, reflection):
    ratio = rows // cols
    own, width = sources.shape[1], sources.shape[2]
    part = -(-own // 16) * 16
    pieces = split_of(width)
    cw = width // pieces
    chunks = ratio * pieces
    r_tile = 256 if cw % 256 == 0 else 128
    traces = cols * part
    src = jnp.pad(sources[0], ((0, part - own), (0, 0)))
    dma, vmem = pltpu.SemaphoreType.DMA, pltpu.VMEM
    result = pl.pallas_call(
        functools.partial(plain_kernel, layers, rows, cols, pieces, r_tile),
        out_shape=jax.ShapeDtypeStruct((part, width), BF16),
        in_specs=[
            pl.BlockSpec(memory_space=pltpu.VMEM),
            pl.BlockSpec(memory_space=pl.ANY),
            pl.BlockSpec(memory_space=pl.ANY),
        ],
        out_specs=pl.BlockSpec(memory_space=pltpu.VMEM),
        scratch_shapes=[
            vmem((chunks, width, cw), BF16),
            vmem((2, width, cw), BF16),
            vmem((cols, pieces, part, cw), BF16),
            vmem((cols, pieces, part, cw), BF16),
            vmem((pieces, cols, part, cw), BF16),
            vmem((chunks, cols, part, cw), BF16),
            vmem((cols, chunks, part, cw), BF16),
            vmem((rows, pieces, part, cw), BF16),
            vmem((pieces, part, cw), BF16),
            vmem((pieces, part, cw), BF16),
            vmem((ratio, pieces, cols, part, cw), BF16),
            vmem((ratio, pieces, cols, part, cw), BF16),
            vmem((width // r_tile, traces, r_tile), F32),
            vmem((cols, pieces, part, cw), BF16),
            vmem((cols, pieces, part, cw), BF16),
            dma((chunks,)), dma((2,)),
            dma((cols,)), dma((cols,)),
            dma((cols, pieces)), dma((cols, pieces)),
            dma((cols, chunks)), dma((cols, chunks)),
            dma((cols, chunks)), dma((rows, pieces)),
            dma((3, pieces, rows)), dma((2, pieces, ratio, cols)),
            dma((cols, pieces)), dma((cols, pieces)),
            pltpu.SemaphoreType.REGULAR,
        ],
        compiler_params=pltpu.CompilerParams(
            collective_id=0, has_side_effects=True, vmem_limit_bytes=66_000_000
        ),
    )(src, transmission[0], reflection[0])
    return result[None, :own]


def solution(mesh):
    sizes = [mesh.shape[name] for name in ("layer", "row", "col")]
    return jax.shard_map(
        functools.partial(per_device, *sizes),
        mesh=mesh,
        in_specs=(P("layer", "col", "row"), P("layer", "row", "col"), P("layer", "row", "col")),
        out_specs=P("layer", "col", "row"),
        check_vma=False,
    )
```
